256 devices in a mesh: dp: 8 (over x, core), seq: 32 (over y, z).
Axes of the slice: x: 4, y: 4, z: 8, core: 2. Of those that a mesh axis runs over, the one named last changes fastest.
Arguments:
- queries: bfloat16 [8, 8192, 4096], P('dp', 'seq'), may hold values from -51 to 51
- keys: bfloat16 [8, 8192, 512], P('dp', 'seq'), may hold values from -6 to 6
- values: bfloat16 [8, 8192, 512], P('dp', 'seq'), may hold values from -6 to 6
- targets: bfloat16 [8, 8192, 4096], P('dp', 'seq'), may hold values from -6 to 6
- q_map: bfloat16 [32, 128, 128], replicated, may hold values from -1.5 to 1.5
- k_map: bfloat16 [4, 128, 128], replicated, may hold values from -1.5 to 1.5
- doc_spans: int32 [8, 8], P('dp'), may hold values from 1 to 24, 64 in all within a row
Outputs:
- grad_q_map: float32 [32, 128, 128], replicated
- grad_k_map: float32 [4, 128, 128], replicated
The draws below stay inside these ranges and needn't reach their ends.
Inputs may be any that keep to these rules, and one draw needn't show every extreme that they name: `doc_spans`: each row sums to 64, and the longest document has exactly 24 blocks.
All inputs are finite; a program needn't handle non-finite values.
Results may differ from the reference program's by a relative error of at most 0.006.
The reference program's roundings to bfloat16 on the way count: a program that leaves them out, or rounds other values in their place, can miss the bound.
Values sent between devices are 32-bit elements; how exact they have to be, the bound alone decides.
A program may use at most 128 MiB of HBM per device.

```python
import math
import jax
import jax.numpy as jnp
import numpy as np
from jax import lax

HQ = 32
HK = 4
HD = 128
SPAN = 128
NDOC = 8
BATCH = 8
LENGTH = 8192
SPANS = 64
MOST_DOC = 24


def draw_queries(key, part):
    shape = (BATCH, LENGTH, HQ * HD)
    base = jax.random.normal(jax.random.fold_in(key, 7), shape, jnp.float32)
    return jnp.clip(base, -6.0, 6.0).astype(jnp.bfloat16)


def block_scale(rng, dims, shards, least, top_value):
    loudness, own = 1.0, jax.random.fold_in(rng, 6)
    for position, blocks in shards:
        draws = jnp.exp(jax.random.uniform(jax.random.fold_in(own, position), (blocks,), jnp.float32, least / len(shards), top_value / len(shards)))
        loudness = loudness * jnp.repeat(draws, dims[position] // blocks).reshape([-1 if axis == position else 1 for axis in range(len(dims))])
    return loudness


def length_profile(number_of, total, limit, slope):
    weights = [(1 << 20) // math.isqrt(standing ** slope) + 1 for standing in range(2, number_of + 1)]
    surplus, given = total - limit - (number_of - 1), [1] * (number_of - 1)
    while surplus > 0:
        free = [i for i in range(number_of - 1) if given[i] < limit]
        whole, remaining = sum([weights[i] for i in free]), surplus
        for i in free:
            more = min(limit - given[i], max(1, remaining * weights[i] // whole), surplus)
            given[i] = given[i] + more
            surplus = surplus - more
    return np.array([limit] + given)


def ragged_sizes(own_key, number_of, total, limit, slope):
    if number_of == 2:
        one = jax.random.randint(own_key, (), max(1, total - limit), min(limit, total - 1) + 1)
        return jnp.stack([one, total - one])
    sizes = jnp.asarray(length_profile(number_of, total, limit, slope), jnp.int32)
    twos = (number_of - 1) // 2
    giver, sink = sizes[1:1 + 2 * twos:2], sizes[2:2 + 2 * twos:2]
    room = jnp.minimum(giver - 1, limit - sink)
    passed = jax.random.randint(jax.random.fold_in(own_key, 1), (twos,), 0, 1 << 20) % (room + 1)
    sizes = sizes.at[1:1 + 2 * twos:2].set(giver - passed).at[2:2 + 2 * twos:2].set(sink + passed)
    return sizes[jax.random.permutation(jax.random.fold_in(own_key, 2), number_of)]


def scatter_about(rng, dims, deviation, most, pieces=(), held_as=jnp.bfloat16):
    result = deviation * jax.random.normal(rng, dims, jnp.float32)
    if pieces:
        result = result * block_scale(rng, dims, pieces, -0.22, 0.18)
    return jnp.clip(result, -most, most).astype(held_as)


def setup_inputs(seed: int = 0) -> dict:
    streams_of = jax.random.split(jax.random.key(seed), 8)
    return {
        "queries": draw_queries(jax.random.fold_in(streams_of[7], 71), 0),
        "keys": scatter_about(streams_of[1], (BATCH, LENGTH, HK * HD), 1.0, 6.0, ((0, 8), (1, 32))),
        "values": scatter_about(streams_of[2], (BATCH, LENGTH, HK * HD), 1.0, 6.0, ((0, 8), (1, 32))),
        "targets": scatter_about(streams_of[3], (BATCH, LENGTH, HQ * HD), 1.0, 6.0, ((0, 8), (1, 32))),
        "q_map": scatter_about(streams_of[4], (HQ, HD, HD), 0.25, 1.5),
        "k_map": scatter_about(streams_of[5], (HK, HD, HD), 0.25, 1.5),
        "doc_spans": jax.vmap(lambda own: ragged_sizes(own, NDOC, SPANS, MOST_DOC, 2))(jax.random.split(streams_of[6], BATCH)).reshape((BATCH, NDOC)).astype(jnp.int32),
    }


def wide(array):
    return array.astype(jnp.float32)

def hedgehog(inputs, weight, form):
    mapped = jnp.einsum(form, wide(inputs), wide(weight), precision=lax.Precision.HIGHEST)
    upper = jax.nn.softmax(mapped, axis=-1)
    lower = jax.nn.softmax(-mapped, axis=-1)
    return (upper, lower, jnp.concatenate([upper, lower], axis=-1).astype(jnp.bfloat16))

def map_grad(upper, lower, grad, width):
    grad_up = grad[..., :width]
    grad_low = grad[..., width:]
    first = upper * (grad_up - lax.optimization_barrier(jnp.sum(upper * grad_up, -1, keepdims=True)))
    second = lower * (grad_low - lax.optimization_barrier(jnp.sum(lower * grad_low, -1, keepdims=True)))
    return (first - second).astype(jnp.bfloat16)

def product(form, left, right):
    return jnp.einsum(form, wide(left), wide(right), precision=lax.Precision.HIGHEST)

def span_middle(feat_q, feat_k, vals, tgt, state_b, norm_b, coef):
    size = feat_q.shape[1]
    causal = jnp.tril(jnp.ones((size, size), jnp.bool_))
    scores = product('ncxgf,nsxf->nxgcs', feat_q, feat_k)
    scores = jnp.where(causal, scores, 0.0)
    local_den = jnp.transpose(lax.optimization_barrier(jnp.sum(scores, -1)), (0, 3, 1, 2))
    numer = product('nxgcs,nsxd->ncxgd', scores.astype(jnp.bfloat16), vals)
    numer = numer + product('ncxgf,nxfd->ncxgd', feat_q, state_b)
    denom = local_den + product('ncxgf,nxf->ncxg', feat_q, norm_b)
    output = numer / denom[..., None]
    d_out = coef * (output - wide(tgt))
    d_numer = (d_out / denom[..., None]).astype(jnp.bfloat16)
    d_denom = -lax.optimization_barrier(jnp.sum(d_out * output, -1)) / denom
    pairs = product('ncxgd,nsxd->nxgcs', d_numer, vals)
    pairs = pairs + jnp.transpose(d_denom, (0, 2, 3, 1))[..., None]
    pairs = jnp.where(causal, pairs, 0.0).astype(jnp.bfloat16)
    d_feat_q = product('nxgcs,nsxf->ncxgf', pairs, feat_k)
    d_feat_q = d_feat_q + product('ncxgd,nxfd->ncxgf', d_numer, state_b)
    d_feat_q = d_feat_q + d_denom[..., None] * wide(norm_b)[:, None, :, None, :]
    back_state = product('ncxgf,ncxgd->nxfd', feat_q, d_numer)
    back_norm = product('ncxgf,ncxg->nxf', feat_q, d_denom)
    return (pairs, d_feat_q, back_state, back_norm)

def span_last(pairs, feat_q, vals, rstate_b, rnorm_b):
    d_feat_k = product('nxgcs,ncxgf->nsxf', pairs, feat_q)
    d_feat_k = d_feat_k + product('nsxd,nxfd->nsxf', vals, rstate_b)
    return d_feat_k + wide(rnorm_b)[:, None, :, :]

def one_sequence(items):
    queries, keys, values, targets, q_map, k_map, lengths = items
    hq = q_map.shape[0]
    hd = q_map.shape[1]
    hk = k_map.shape[0]
    group = hq // hk
    count = queries.shape[0] // SPAN
    coef = 2.0 / math.sqrt(BATCH * LENGTH * HD)
    q_heads = queries.reshape(count, SPAN, hq, hd)
    k_heads = keys.reshape(count, SPAN, hk, hd)
    vals = values.reshape(count, SPAN, hk, hd)
    tgt = targets.reshape(count, SPAN, hk, group, hd)
    q_up, q_low, feat_q = hedgehog(q_heads, q_map, 'ncxd,xde->ncxe')
    k_up, k_low, feat_k = hedgehog(k_heads, k_map, 'ncxd,xde->ncxe')
    feat_q = feat_q.reshape(count, SPAN, hk, group, 2 * hd)
    starts = jnp.cumsum(lengths) - lengths
    span_ids = jnp.arange(count, dtype=jnp.int32)
    opens = jnp.any(span_ids[:, None] == starts[None, :].astype(jnp.int32), axis=1)
    key_state = product('ncxf,ncxd->nxfd', feat_k, vals)
    key_norm = lax.optimization_barrier(jnp.sum(wide(feat_k), axis=1))

    def forward_step(carry, item):
        state, norm = carry
        add_state, add_norm, reset = item
        state = jnp.where(reset, 0.0, state)
        norm = jnp.where(reset, 0.0, norm)
        return ((state + add_state, norm + add_norm), (state, norm))
    zero_state = jnp.zeros(key_state.shape[1:], key_state.dtype)
    zero_norm = jnp.zeros(key_norm.shape[1:], key_norm.dtype)
    _, (state, norm) = lax.scan(forward_step, (zero_state, zero_norm), (key_state, key_norm, opens))
    pairs, d_feat_q, back_state, back_norm = span_middle(feat_q, feat_k, vals, tgt, state.astype(jnp.bfloat16), norm.astype(jnp.bfloat16), coef)

    def reverse_step(carry, item):
        state_r, norm_r = carry
        add_state, add_norm, reset = item
        out = (state_r, norm_r)
        state_r = jnp.where(reset, 0.0, state_r + add_state)
        norm_r = jnp.where(reset, 0.0, norm_r + add_norm)
        return ((state_r, norm_r), out)
    zero_rstate = jnp.zeros(back_state.shape[1:], back_state.dtype)
    zero_rnorm = jnp.zeros(back_norm.shape[1:], back_norm.dtype)
    _, (rstate, rnorm) = lax.scan(reverse_step, (zero_rstate, zero_rnorm), (back_state, back_norm, opens), reverse=True)
    d_feat_k = span_last(pairs, feat_q, vals, rstate.astype(jnp.bfloat16), rnorm.astype(jnp.bfloat16))
    du_q = map_grad(q_up, q_low, d_feat_q.reshape(count, SPAN, hq, 2 * hd), hd)
    du_k = map_grad(k_up, k_low, d_feat_k, hd)
    grad_q = product('ncxd,ncxe->xde', q_heads, du_q)
    grad_k = product('ncxd,ncxe->xde', k_heads, du_k)
    return (grad_q, grad_k)

def reference(queries, keys, values, targets, q_map, k_map, doc_spans):
    batch = queries.shape[0]
    q_maps = jnp.broadcast_to(q_map[None], (batch,) + q_map.shape)
    k_maps = jnp.broadcast_to(k_map[None], (batch,) + k_map.shape)
    grad_q, grad_k = lax.map(one_sequence, (queries, keys, values, targets, q_maps, k_maps, doc_spans))
    return (lax.optimization_barrier(jnp.sum(grad_q, axis=0)), lax.optimization_barrier(jnp.sum(grad_k, axis=0)))
```

```python
import functools
import math

import jax
import jax.numpy as jnp
from jax import lax
from jax.experimental import pallas as pl
from jax.experimental.pallas import tpu as pltpu
from jax.sharding import PartitionSpec as P

MESH = pl.DeviceIdType.MESH
F32 = jnp.float32
BF16 = jnp.bfloat16
SPAN = 128
HD = 128
HK = 4
GROUP = 8
NDOC = 8
NZ = 8
NY = 4
NDP = 8
SLICE = 136
ROWS = NZ * SLICE
ZROW = HK * 256


def dot(a, b, ca, cb):
    return lax.dot_general(a, b, (((ca,), (cb,)), ((), ())), preferred_element_type=F32)


def starts_of(spans_ref):
    starts, total = [], jnp.int32(0)
    for n in range(NDOC):
        starts.append(total)
        total = total + spans_ref[0, n]
    return starts


def no_start(starts, *blocks):
    hit = jnp.bool_(False)
    for s in starts:
        for b in blocks:
            hit = jnp.logical_or(hit, s == b)
    return jnp.where(hit, 0.0, 1.0).astype(F32)


def softmax_pair(u):
    e1 = jnp.exp(u - jnp.max(u, -1, keepdims=True))
    e2 = jnp.exp(jnp.min(u, -1, keepdims=True) - u)
    p1 = e1 * (1.0 / jnp.sum(e1, -1, keepdims=True))
    p2 = e2 * (1.0 / jnp.sum(e2, -1, keepdims=True))
    return p1, p2


def map_grad(p1, p2, d1, d2):
    s1 = jnp.sum(p1 * d1, -1, keepdims=True)
    s2 = jnp.sum(p2 * d2, -1, keepdims=True)
    return (p1 * (d1 - s1) - p2 * (d2 - s2)).astype(BF16)


def key_kernel(spans_ref, k_ref, v_ref, w_ref, fk_ref, pk_ref, st0_ref, sum_ref, co_ref):
    seq = lax.axis_index("seq")
    y = seq // NZ
    starts = starts_of(spans_ref)
    same = no_start(starts, 2 * seq + 1)
    st0_ref[pl.ds(ZROW, ROWS - ZROW), :] = jnp.zeros((ROWS - ZROW, 128), F32)
    sum_ref[pl.ds(ZROW, ROWS - ZROW), :] = jnp.zeros((ROWS - ZROW, 128), F32)
    for h in range(HK):
        cols = slice(h * HD, (h + 1) * HD)
        u = dot(k_ref[:, cols], w_ref[h], 1, 0)
        p1, p2 = softmax_pair(u)
        pk_ref[0, :, cols] = p1
        pk_ref[1, :, cols] = p2
        fk = jnp.concatenate([p1, p2], -1).astype(BF16)
        fk_ref[:, h * 256 : (h + 1) * 256] = fk
        v = v_ref[:, cols]
        st = [dot(v[c * SPAN : (c + 1) * SPAN], fk[c * SPAN : (c + 1) * SPAN], 0, 0) for c in (0, 1)]
        zs = [jnp.sum(fk[c * SPAN : (c + 1) * SPAN].astype(F32), 0, keepdims=True) for c in (0, 1)]
        for half in (0, 1):
            part = slice(half * 128, (half + 1) * 128)
            rows = pl.ds(h * 256 + half * 128, 128)
            st0_ref[rows, :] = st[0][:, part]
            sum_ref[rows, :] = same * st[0][:, part] + st[1][:, part]
            zr = pl.ds(ZROW + 2 * h + half, 1)
            st0_ref[zr, :] = zs[0][:, part]
            sum_ref[zr, :] = same * zs[0][:, part] + zs[1][:, part]
    pos = lax.broadcasted_iota(jnp.int32, (NZ, 128), 0) + y * NZ
    hit = jnp.zeros((NZ, 128), F32)
    for s in starts:
        hit = jnp.where(pos == s // 2, 1.0, hit)
    co_ref[0:8, :] = 1.0 - hit
    last = jnp.float32(1.0)
    nxt = jnp.float32(1.0)
    for s in starts:
        last = jnp.where(s // 16 == y - 1, 0.0, last)
        nxt = jnp.where(s // 16 == y + 1, 0.0, nxt)
    co_ref[8:9, :] = jnp.full((1, 128), jnp.where(y >= 1, 1.0, 0.0), F32)
    co_ref[9:10, :] = jnp.full((1, 128), jnp.where(y >= 2, last, 0.0), F32)
    co_ref[10:11, :] = jnp.full((1, 128), jnp.where(y <= 2, 1.0, 0.0), F32)
    co_ref[11:12, :] = jnp.full((1, 128), jnp.where(y <= 1, nxt, 0.0), F32)
    co_ref[12:16, :] = jnp.zeros((4, 128), F32)


def remote(src, dst, send, recv, dev):
    return pltpu.make_async_remote_copy(
        src_ref=src, dst_ref=dst, send_sem=send, recv_sem=recv, device_id=dev, device_id_type=MESH
    )


def rows_of(index, size):
    return pl.ds(pl.multiple_of(index * size, 8), size)


def where_am_i():
    dp = lax.axis_index("dp")
    seq = lax.axis_index("seq")
    return dp, seq, lax.div(seq, NZ), lax.rem(seq, NZ)


def greet(peers):
    barrier = pltpu.get_barrier_semaphore()
    for dev in peers:
        pl.semaphore_signal(barrier, inc=1, device_id=dev, device_id_type=MESH)
    pl.semaphore_wait(barrier, len(peers))


def z_peers(dp, y, z):
    return [(dp, y * NZ + lax.rem(z + d, NZ)) for d in range(1, NZ)]


def y_peers(dp, y, z):
    return [(dp, lax.rem(y + d, NY) * NZ + z) for d in range(1, NY)]


def scan_scratch():
    return [
        pltpu.VMEM((NZ, SLICE, 128), F32),
        pltpu.VMEM((SLICE, 128), F32),
        pltpu.VMEM((2, SLICE, 128), F32),
        pltpu.VMEM((NZ, SLICE, 128), F32),
        pltpu.SemaphoreType.DMA((2, NZ)),
        pltpu.SemaphoreType.DMA((2, 2)),
        pltpu.SemaphoreType.DMA((2, NZ)),
    ]


class Scan:
    def __init__(self, own, out, co, scratch, reverse):
        self.own, self.out, self.co, self.reverse = own, out, co, reverse
        self.seen, self.total, self.rows_in, self.back, self.s1, self.s2, self.s3 = scratch
        self.dp, self.seq, self.y, self.z = where_am_i()

    def start(self):
        self.copies = []
        for d in range(1, NZ):
            to = lax.rem(self.z + d, NZ)
            copy = remote(
                self.own.at[rows_of(to, SLICE)],
                self.seen.at[self.z],
                self.s1.at[0, d],
                self.s1.at[1, d],
                (self.dp, self.y * NZ + to),
            )
            copy.start()
            self.copies.append(copy)

    def totals(self):
        self.seen[self.z] = self.own[rows_of(self.z, SLICE), :]
        for copy in self.copies:
            copy.wait_recv()
        order = list(range(NZ))[::-1] if self.reverse else list(range(NZ))
        acc = jnp.zeros((SLICE, 128), F32)
        for k in order:
            self.back[k] = acc
            acc = self.seen[k] + self.co[k : k + 1, :] * acc
        self.total[...] = acc
        self.row_copies = []
        for d in (1, 2):
            step = NY - d if self.reverse else d
            copy = remote(
                self.total,
                self.rows_in.at[d - 1],
                self.s2.at[0, d - 1],
                self.s2.at[1, d - 1],
                (self.dp, lax.rem(self.y + step, NY) * NZ + self.z),
            )
            copy.start()
            self.row_copies.append(copy)

    def give_back(self):
        for copy in self.row_copies:
            copy.wait_recv()
        first = 10 if self.reverse else 8
        carry = (
            self.co[first : first + 1, :] * self.rows_in[0]
            + self.co[first + 1 : first + 2, :] * self.rows_in[1]
        )
        order = list(range(NZ))[::-1] if self.reverse else list(range(NZ))
        keep = jnp.ones((1, 128), F32)
        for k in order:
            self.back[k] = self.back[k] + keep * carry
            keep = keep * self.co[k : k + 1, :]
        self.out[rows_of(self.z, SLICE), :] = self.back[self.z]
        self.back_copies = []
        for d in range(1, NZ):
            to = lax.rem(self.z + d, NZ)
            copy = remote(
                self.back.at[to],
                self.out.at[rows_of(self.z, SLICE)],
                self.s3.at[0, d],
                self.s3.at[1, d],
                (self.dp, self.y * NZ + to),
            )
            copy.start()
            self.back_copies.append(copy)

    def arrived(self):
        for copy in self.back_copies:
            copy.wait_recv()

    def finish(self):
        for copy in self.copies + self.row_copies + self.back_copies:
            copy.wait_send()


def state_kernel(own_ref, co_ref, out_ref, *scratch):
    dp, seq, y, z = where_am_i()
    greet(z_peers(dp, y, z) + y_peers(dp, y, z))
    scan = Scan(own_ref, out_ref, co_ref, scratch, False)
    scan.start()
    scan.totals()
    scan.give_back()
    scan.arrived()
    scan.finish()


def middle_kernel(
    coef, spans_ref, q_ref, t_ref, v_ref, fk_ref, w_ref, st0_ref, st0z_ref, in_ref, inz_ref,
    gq_ref, back_ref, back1_ref, dfk_ref, fq_s, x_s, p_s, m_s,
):
    head = pl.program_id(0)
    block = pl.program_id(1)
    seq = lax.axis_index("seq")
    starts = starts_of(spans_ref)
    b0 = 2 * seq
    in0 = no_start(starts, b0)
    same = no_start(starts, b0 + 1)
    in1 = no_start(starts, b0, b0 + 1)
    w_in = jnp.where(block == 0, in0, in1)
    w_st = jnp.where(block == 0, 0.0, same)
    m_s[0:128, :] = fk_ref[...]
    zb = []
    for half in (0, 1):
        rows = slice(half * 128, (half + 1) * 128)
        m_s[128:256, rows] = (w_in * in_ref[rows, :] + w_st * st0_ref[rows, :]).astype(BF16)
        zr = pl.ds(2 * head + half, 1)
        zb.append((w_in * inz_ref[zr, :] + w_st * st0z_ref[zr, :]).astype(BF16).astype(F32))
    m = m_s[...]
    v = v_ref[...]
    causal = lax.broadcasted_iota(jnp.int32, (SPAN, SPAN), 0) >= lax.broadcasted_iota(
        jnp.int32, (SPAN, SPAN), 1
    )
    gz = [jnp.zeros((8, 128), F32), jnp.zeros((8, 128), F32)]
    for g in range(GROUP):
        cols = slice(g * HD, (g + 1) * HD)
        rows = slice(g * SPAN, (g + 1) * SPAN)
        q = q_ref[:, cols]
        p1, p2 = softmax_pair(dot(q, w_ref[g], 1, 0))
        f1 = p1.astype(BF16)
        f2 = p2.astype(BF16)
        fq_s[rows, 0:128] = f1
        fq_s[rows, 128:256] = f2
        p_s[g % 2, 0] = p1
        p_s[g % 2, 1] = p2
        both = dot(fq_s[rows, :], m, 1, 1)
        scores = jnp.where(causal, both[:, 0:128], 0.0)
        f1 = f1.astype(F32)
        f2 = f2.astype(F32)
        den = jnp.sum(scores + f1 * zb[0] + f2 * zb[1], -1, keepdims=True)
        inv = 1.0 / den
        num = dot(scores.astype(BF16), v, 1, 0) + both[:, 128:256]
        out = num * inv
        dy = coef * (out - t_ref[:, cols].astype(F32))
        dnum = (dy * inv).astype(BF16)
        dden = -jnp.sum(dy * out, -1, keepdims=True) * inv
        pairs = jnp.where(causal, dot(dnum, v, 1, 1) + dden, 0.0).astype(BF16)
        x_s[rows, 0:128] = pairs
        x_s[rows, 128:256] = dnum
        for half, f in ((0, f1), (1, f2)):
            gz[half] = gz[half] + jnp.sum((f * dden).reshape(SPAN // 8, 8, 128), 0)
        dfq = dot(x_s[rows, :], m, 1, 0)
        duq = map_grad(
            p_s[g % 2, 0], p_s[g % 2, 1], dfq[:, 0:128] + dden * zb[0], dfq[:, 128:256] + dden * zb[1]
        )
        grad = dot(q, duq, 0, 0)

        @pl.when(block == 0)
        def _():
            gq_ref[g] = grad

        @pl.when(block == 1)
        def _():
            gq_ref[g] = gq_ref[g] + grad

    acc = dot(x_s[...], fq_s[...], 0, 0)
    dfk_ref[...] = acc[0:128, :]

    @pl.when(jnp.logical_and(head == 0, block == 0))
    def _():
        back_ref[pl.ds(ZROW, ROWS - ZROW), :] = jnp.zeros((ROWS - ZROW, 128), F32)
        back1_ref[pl.ds(ZROW, ROWS - ZROW), :] = jnp.zeros((ROWS - ZROW, 128), F32)

    for half in (0, 1):
        part = acc[128:256, half * 128 : (half + 1) * 128]
        zpart = jnp.sum(gz[half], 0, keepdims=True)
        rows = pl.ds(pl.multiple_of(head * 256 + half * 128, 128), 128)
        zr = pl.ds(ZROW + 2 * head + half, 1)

        @pl.when(block == 0)
        def _():
            back_ref[rows, :] = in0 * part
            back_ref[zr, :] = in0 * zpart

        @pl.when(block == 1)
        def _():
            back_ref[rows, :] = back_ref[rows, :] + in1 * part
            back_ref[zr, :] = back_ref[zr, :] + in1 * zpart
            back1_ref[rows, :] = part
            back1_ref[zr, :] = zpart


def send_all(items):
    copies = [remote(*item) for item in items]
    for copy in copies:
        copy.start()
    return copies


def last_kernel(
    spans_ref, own_ref, co_ref, back1_ref, dfk_ref, pk_ref, k_ref, v_ref, gq_ref,
    oq_ref, ok_ref, rin, half_in, half, xy_in, quarter, z_in, gk, kd_in, kd, ky_in, ky, kz_in,
    sc, sxy, sz, az, axy, ac, skd, sky, skz, aky, akd, *scratch,
):
    dp, seq, y, z = where_am_i()
    x, core = lax.div(dp, 2), lax.rem(dp, 2)

    def plane(d):
        px, py = lax.rem(x + d // 4, 4), lax.rem(y + d % 4, 4)
        return px, py, (px * 2 + core, py * NZ + z)

    mate = (x * 2 + (1 - core), seq)
    zs = z_peers(dp, y, z)
    dps = [(lax.rem(dp + d, NDP), seq) for d in range(1, NDP)]
    planes = [plane(d)[2] for d in range(1, 16)]
    other = [(lax.rem(x + d, 4) * 2 + (1 - core), seq) for d in range(4)]
    greet(zs + planes + other)

    scan = Scan(own_ref, rin, co_ref, scratch, True)
    scan.start()
    pair = send_all([(gq_ref.at[rows_of(1 - core, 2048)], half_in, sc.at[0], sc.at[1], mate)])
    pair[0].wait_recv()
    half[...] = gq_ref[rows_of(core, 2048), :] + half_in[...]
    spread = []
    for d in range(1, 16):
        px, py, dev = plane(d)
        spread.append((half.at[rows_of(px * 4 + py, 128)], xy_in.at[d], sxy.at[0, d], sxy.at[1, d], dev))
    spread = send_all(spread)
    scan.totals()
    scan.give_back()
    for copy in spread:
        copy.wait_recv()
    me_xy = x * 4 + y
    acc = half[rows_of(me_xy, 128), :]
    for d in range(1, 16):
        acc = acc + xy_in[d]
    quarter[...] = acc
    base = core * 2048 + me_xy * 128
    zsend = send_all([
        (quarter.at[rows_of(lax.rem(z + d, NZ), 16)], z_in.at[d], sz.at[0, d], sz.at[1, d], zs[d - 1])
        for d in range(1, NZ)
    ])
    scan.arrived()

    starts = starts_of(spans_ref)
    b0 = 2 * seq
    same = no_start(starts, b0 + 1)
    out0 = no_start(starts, b0 + 1, b0 + 2)
    out1 = no_start(starts, b0 + 2)
    for h in range(HK):
        cols = slice(h * HD, (h + 1) * HD)
        total = jnp.zeros((HD, HD), F32)
        for c in (0, 1):
            toks = slice(c * SPAN, (c + 1) * SPAN)
            grads = []
            for hf in (0, 1):
                rows = slice(h * 256 + hf * 128, h * 256 + (hf + 1) * 128)
                zr = slice(ZROW + 2 * h + hf, ZROW + 2 * h + hf + 1)
                if c == 0:
                    r = same * back1_ref[rows, :] + out0 * rin[rows, :]
                    rz = same * back1_ref[zr, :] + out0 * rin[zr, :]
                else:
                    r = out1 * rin[rows, :]
                    rz = out1 * rin[zr, :]
                f = slice(h * 256 + hf * 128, h * 256 + (hf + 1) * 128)
                grads.append(
                    dfk_ref[toks, f] + dot(v_ref[toks, cols], r.astype(BF16), 1, 0)
                    + rz.astype(BF16).astype(F32)
                )
            duk = map_grad(pk_ref[0, toks, cols], pk_ref[1, toks, cols], grads[0], grads[1])
            total = total + dot(k_ref[toks, cols], duk, 0, 0)
        gk[h * HD : (h + 1) * HD, :] = total
    kdsend = send_all([
        (gk.at[rows_of(lax.rem(dp + d, NDP), 64)], kd_in.at[d], skd.at[0, d], skd.at[1, d], dps[d - 1])
        for d in range(1, NDP)
    ])

    for copy in zsend:
        copy.wait_recv()
    acc = quarter[rows_of(z, 16), :]
    for d in range(1, NZ):
        acc = acc + z_in[d]
    mine = pl.ds(pl.multiple_of(base + z * 16, 8), 16)
    oq_ref[mine, :] = acc
    zback = send_all([
        (oq_ref.at[mine], oq_ref.at[mine], az.at[0, d], az.at[1, d], zs[d - 1]) for d in range(1, NZ)
    ])

    for copy in kdsend:
        copy.wait_recv()
    acc = gk[rows_of(dp, 64), :]
    for d in range(1, NDP):
        acc = acc + kd_in[d]
    kd[...] = acc
    ys = y_peers(dp, y, z)
    kysend = send_all([
        (kd.at[rows_of(lax.rem(y + d, NY), 16)], ky_in.at[d], sky.at[0, d], sky.at[1, d], ys[d - 1])
        for d in range(1, NY)
    ])

    for copy in zback:
        copy.wait_recv()
    block = pl.ds(pl.multiple_of(base, 128), 128)
    xyback = send_all([
        (oq_ref.at[block], oq_ref.at[block], axy.at[0, d], axy.at[1, d], planes[d - 1])
        for d in range(1, 16)
    ])

    for copy in kysend:
        copy.wait_recv()
    acc = kd[rows_of(y, 16), :]
    for d in range(1, NY):
        acc = acc + ky_in[d]
    ky[...] = acc
    kz_in[z] = acc
    kzsend = send_all([
        (ky, kz_in.at[z], skz.at[0, d], skz.at[1, d], zs[d - 1]) for d in range(1, NZ)
    ])
    for copy in kzsend:
        copy.wait_recv()
    acc = kz_in[0]
    for k in range(1, NZ):
        acc = acc + kz_in[k]
    kmine = pl.ds(pl.multiple_of(dp * 64 + y * 16, 8), 16)
    ok_ref[kmine, :] = acc
    kyback = send_all([
        (ok_ref.at[kmine], ok_ref.at[kmine], aky.at[0, d], aky.at[1, d], ys[d - 1]) for d in range(1, NY)
    ])
    for copy in kyback:
        copy.wait_recv()
    kblock = rows_of(dp, 64)
    kdback = send_all([
        (ok_ref.at[kblock], ok_ref.at[kblock], akd.at[0, d], akd.at[1, d], dps[d - 1])
        for d in range(1, NDP)
    ])

    for copy in xyback:
        copy.wait_recv()
    whole = rows_of(core, 2048)
    back = send_all([(oq_ref.at[whole], oq_ref.at[whole], ac.at[0], ac.at[1], mate)])
    for copy in kdback + back:
        copy.wait_recv()
    scan.finish()
    for copy in pair + spread + zsend + kdsend + zback + kysend + xyback + kzsend + kyback + kdback + back:
        copy.wait_send()


VM = pl.BlockSpec(memory_space=pltpu.VMEM)
SM = pl.BlockSpec(memory_space=pltpu.SMEM)
LIMIT = 56 * 1024 * 1024


def shape(dims, dtype=F32):
    return jax.ShapeDtypeStruct(dims, dtype)


def shards(queries, keys, values, targets, q_map, k_map, doc_spans):
    q, t = queries[0], targets[0]
    k, v = keys[0], values[0]
    toks = q.shape[0]
    coef = 2.0 / math.sqrt(lax.axis_size("dp") * lax.axis_size("seq") * toks * HD)
    fk, pk, st0, own, co = pl.pallas_call(
        key_kernel,
        out_shape=(
            shape((toks, HK * 256), BF16), shape((2, toks, HK * HD)), shape((ROWS, 128)),
            shape((ROWS, 128)), shape((16, 128)),
        ),
        in_specs=[SM, VM, VM, VM],
        out_specs=(VM,) * 5,
        compiler_params=pltpu.CompilerParams(vmem_limit_bytes=LIMIT),
        name="keys",
    )(doc_spans, k, v, k_map)

    state_in = pl.pallas_call(
        state_kernel,
        out_shape=shape((ROWS, 128)),
        in_specs=[VM, VM],
        out_specs=VM,
        scratch_shapes=scan_scratch(),
        compiler_params=pltpu.CompilerParams(
            collective_id=0, has_side_effects=True, vmem_limit_bytes=LIMIT
        ),
        name="scan",
    )(own, co)

    head_rows = pl.BlockSpec((256, 128), lambda i, c: (i, 0))
    z_rows = pl.BlockSpec((8, 128), lambda i, c: (ZROW // 8, 0))
    whole = pl.BlockSpec((ROWS, 128), lambda i, c: (0, 0))
    gq, back, back1, dfk = pl.pallas_call(
        functools.partial(middle_kernel, coef),
        grid=(HK, 2),
        out_shape=(
            shape((HK * GROUP, HD, HD)), shape((ROWS, 128)), shape((ROWS, 128)), shape((toks, HK * 256)),
        ),
        in_specs=[
            SM,
            pl.BlockSpec((SPAN, GROUP * HD), lambda i, c: (c, i)),
            pl.BlockSpec((SPAN, GROUP * HD), lambda i, c: (c, i)),
            pl.BlockSpec((SPAN, HD), lambda i, c: (c, i)),
            pl.BlockSpec((SPAN, 256), lambda i, c: (c, i)),
            pl.BlockSpec((GROUP, HD, HD), lambda i, c: (i, 0, 0)),
            head_rows, z_rows, head_rows, z_rows,
        ],
        out_specs=(
            pl.BlockSpec((GROUP, HD, HD), lambda i, c: (i, 0, 0)),
            whole, whole,
            pl.BlockSpec((SPAN, 256), lambda i, c: (c, i)),
        ),
        scratch_shapes=[
            pltpu.VMEM((GROUP * SPAN, 256), BF16),
            pltpu.VMEM((GROUP * SPAN, 256), BF16),
            pltpu.VMEM((2, 2, SPAN, 128), F32),
            pltpu.VMEM((256, 256), BF16),
        ],
        compiler_params=pltpu.CompilerParams(
            dimension_semantics=("arbitrary", "arbitrary"), vmem_limit_bytes=LIMIT
        ),
        name="middle",
    )(doc_spans, q, t, v, fk, q_map, st0, st0, state_in, state_in)

    dma = pltpu.SemaphoreType.DMA
    gq, gk = pl.pallas_call(
        last_kernel,
        out_shape=(shape((HK * GROUP * HD, HD)), shape((HK * HD, HD))),
        in_specs=[SM] + [VM] * 8,
        out_specs=(VM, VM),
        scratch_shapes=[
            pltpu.VMEM((ROWS, 128), F32),
            pltpu.VMEM((2048, 128), F32),
            pltpu.VMEM((2048, 128), F32),
            pltpu.VMEM((16, 128, 128), F32),
            pltpu.VMEM((128, 128), F32),
            pltpu.VMEM((NZ, 16, 128), F32),
            pltpu.VMEM((HK * HD, 128), F32),
            pltpu.VMEM((NDP, 64, 128), F32),
            pltpu.VMEM((64, 128), F32),
            pltpu.VMEM((NY, 16, 128), F32),
            pltpu.VMEM((16, 128), F32),
            pltpu.VMEM((NZ, 16, 128), F32),
            dma((2,)), dma((2, 16)), dma((2, NZ)), dma((2, NZ)), dma((2, 16)), dma((2,)),
            dma((2, NDP)), dma((2, NY)), dma((2, NZ)), dma((2, NY)), dma((2, NDP)),
        ] + scan_scratch(),
        compiler_params=pltpu.CompilerParams(
            collective_id=1, has_side_effects=True, vmem_limit_bytes=LIMIT
        ),
        name="last",
    )(doc_spans, back, co, back1, dfk, pk, k, v, gq.reshape(HK * GROUP * HD, HD))
    return gq.reshape(HK * GROUP, HD, HD), gk.reshape(HK, HD, HD)


def solution(mesh):
    placed = (
        P("dp", "seq", None), P("dp", "seq", None), P("dp", "seq", None), P("dp", "seq", None),
        P(), P(), P("dp", None),
    )
    return jax.shard_map(shards, mesh=mesh, in_specs=placed, out_specs=(P(), P()), check_vma=False)
```

```python
import functools
import math

import jax
import jax.numpy as jnp
from jax import lax
from jax.experimental import pallas as pl
from jax.experimental.pallas import tpu as pltpu
from jax.sharding import PartitionSpec as P

MESH = pl.DeviceIdType.MESH
F32 = jnp.float32
BF16 = jnp.bfloat16
SPAN = 128
HD = 128
HK = 4
GROUP = 8
NDOC = 8
NZ = 8
NY = 4
NDP = 8
SLICE = 136
ROWS = NZ * SLICE
ZROW = HK * 256


def dot(a, b, ca, cb):
    return lax.dot_general(a, b, (((ca,), (cb,)), ((), ())), preferred_element_type=F32)


def starts_of(spans_ref):
    starts, total = [], jnp.int32(0)
    for n in range(NDOC):
        starts.append(total)
        total = total + spans_ref[0, n]
    return starts


def no_start(starts, *blocks):
    hit = jnp.bool_(False)
    for s in starts:
        for b in blocks:
            hit = jnp.logical_or(hit, s == b)
    return jnp.where(hit, 0.0, 1.0).astype(F32)


def softmax_pair(u):
    e1 = jnp.exp(u - jnp.max(u, -1, keepdims=True))
    e2 = jnp.exp(jnp.min(u, -1, keepdims=True) - u)
    p1 = e1 * (1.0 / jnp.sum(e1, -1, keepdims=True))
    p2 = e2 * (1.0 / jnp.sum(e2, -1, keepdims=True))
    return p1, p2


def map_grad(p1, p2, d1, d2):
    s1 = jnp.sum(p1 * d1, -1, keepdims=True)
    s2 = jnp.sum(p2 * d2, -1, keepdims=True)
    return (p1 * (d1 - s1) - p2 * (d2 - s2)).astype(BF16)


def key_kernel(spans_ref, k_ref, v_ref, w_ref, fk_ref, pk_ref, st0_ref, sum_ref, co_ref):
    seq = lax.axis_index("seq")
    y = seq // NZ
    starts = starts_of(spans_ref)
    same = no_start(starts, 2 * seq + 1)
    st0_ref[pl.ds(ZROW, ROWS - ZROW), :] = jnp.zeros((ROWS - ZROW, 128), F32)
    sum_ref[pl.ds(ZROW, ROWS - ZROW), :] = jnp.zeros((ROWS - ZROW, 128), F32)
    for h in range(HK):
        cols = slice(h * HD, (h + 1) * HD)
        u = dot(k_ref[:, cols], w_ref[h], 1, 0)
        p1, p2 = softmax_pair(u)
        pk_ref[0, :, cols] = p1
        pk_ref[1, :, cols] = p2
        fk = jnp.concatenate([p1, p2], -1).astype(BF16)
        fk_ref[:, h * 256 : (h + 1) * 256] = fk
        v = v_ref[:, cols]
        st = [dot(v[c * SPAN : (c + 1) * SPAN], fk[c * SPAN : (c + 1) * SPAN], 0, 0) for c in (0, 1)]
        zs = [jnp.sum(fk[c * SPAN : (c + 1) * SPAN].astype(F32), 0, keepdims=True) for c in (0, 1)]
        for half in (0, 1):
            part = slice(half * 128, (half + 1) * 128)
            rows = pl.ds(h * 256 + half * 128, 128)
            st0_ref[rows, :] = st[0][:, part]
            sum_ref[rows, :] = same * st[0][:, part] + st[1][:, part]
            zr = pl.ds(ZROW + 2 * h + half, 1)
            st0_ref[zr, :] = zs[0][:, part]
            sum_ref[zr, :] = same * zs[0][:, part] + zs[1][:, part]
    pos = lax.broadcasted_iota(jnp.int32, (NZ, 128), 0) + y * NZ
    hit = jnp.zeros((NZ, 128), F32)
    for s in starts:
        hit = jnp.where(pos == s // 2, 1.0, hit)
    co_ref[0:8, :] = 1.0 - hit
    last = jnp.float32(1.0)
    nxt = jnp.float32(1.0)
    for s in starts:
        last = jnp.where(s // 16 == y - 1, 0.0, last)
        nxt = jnp.where(s // 16 == y + 1, 0.0, nxt)
    co_ref[8:9, :] = jnp.full((1, 128), jnp.where(y >= 1, 1.0, 0.0), F32)
    co_ref[9:10, :] = jnp.full((1, 128), jnp.where(y >= 2, last, 0.0), F32)
    co_ref[10:11, :] = jnp.full((1, 128), jnp.where(y <= 2, 1.0, 0.0), F32)
    co_ref[11:12, :] = jnp.full((1, 128), jnp.where(y <= 1, nxt, 0.0), F32)
    co_ref[12:16, :] = jnp.zeros((4, 128), F32)


def remote(src, dst, send, recv, dev):
    return pltpu.make_async_remote_copy(
        src_ref=src, dst_ref=dst, send_sem=send, recv_sem=recv, device_id=dev, device_id_type=MESH
    )


def rows_of(index, size):
    return pl.ds(pl.multiple_of(index * size, 8), size)


def where_am_i():
    dp = lax.axis_index("dp")
    seq = lax.axis_index("seq")
    return dp, seq, lax.div(seq, NZ), lax.rem(seq, NZ)


def greet(peers):
    barrier = pltpu.get_barrier_semaphore()
    for dev in peers:
        pl.semaphore_signal(barrier, inc=1, device_id=dev, device_id_type=MESH)
    pl.semaphore_wait(barrier, len(peers))


def z_peers(dp, y, z):
    return [(dp, y * NZ + lax.rem(z + d, NZ)) for d in range(1, NZ)]


def y_peers(dp, y, z):
    return [(dp, lax.rem(y + d, NY) * NZ + z) for d in range(1, NY)]


def scan_scratch():
    return [
        pltpu.VMEM((NZ, SLICE, 128), F32),
        pltpu.VMEM((SLICE, 128), F32),
        pltpu.VMEM((2, SLICE, 128), F32),
        pltpu.VMEM((NZ, SLICE, 128), F32),
        pltpu.SemaphoreType.DMA((2, NZ)),
        pltpu.SemaphoreType.DMA((2, 2)),
        pltpu.SemaphoreType.DMA((2, NZ)),
    ]


class Scan:
    def __init__(self, own, out, co, scratch, reverse):
        self.own, self.out, self.co, self.reverse = own, out, co, reverse
        self.seen, self.total, self.rows_in, self.back, self.s1, self.s2, self.s3 = scratch
        self.dp, self.seq, self.y, self.z = where_am_i()

    def start(self):
        self.copies = []
        for d in range(1, NZ):
            to = lax.rem(self.z + d, NZ)
            copy = remote(
                self.own.at[rows_of(to, SLICE)],
                self.seen.at[self.z],
                self.s1.at[0, d],
                self.s1.at[1, d],
                (self.dp, self.y * NZ + to),
            )
            copy.start()
            self.copies.append(copy)

    def totals(self):
        self.seen[self.z] = self.own[rows_of(self.z, SLICE), :]
        for copy in self.copies:
            copy.wait_recv()
        order = list(range(NZ))[::-1] if self.reverse else list(range(NZ))
        acc = jnp.zeros((SLICE, 128), F32)
        for k in order:
            self.back[k] = acc
            acc = self.seen[k] + self.co[k : k + 1, :] * acc
        self.total[...] = acc
        self.row_copies = []
        for d in (1, 2):
            step = NY - d if self.reverse else d
            copy = remote(
                self.total,
                self.rows_in.at[d - 1],
                self.s2.at[0, d - 1],
                self.s2.at[1, d - 1],
                (self.dp, lax.rem(self.y + step, NY) * NZ + self.z),
            )
            copy.start()
            self.row_copies.append(copy)

    def give_back(self):
        for copy in self.row_copies:
            copy.wait_recv()
        first = 10 if self.reverse else 8
        carry = (
            self.co[first : first + 1, :] * self.rows_in[0]
            + self.co[first + 1 : first + 2, :] * self.rows_in[1]
        )
        order = list(range(NZ))[::-1] if self.reverse else list(range(NZ))
        keep = jnp.ones((1, 128), F32)
        for k in order:
            self.back[k] = self.back[k] + keep * carry
            keep = keep * self.co[k : k + 1, :]
        self.out[rows_of(self.z, SLICE), :] = self.back[self.z]
        self.back_copies = []
        for d in range(1, NZ):
            to = lax.rem(self.z + d, NZ)
            copy = remote(
                self.back.at[to],
                self.out.at[rows_of(self.z, SLICE)],
                self.s3.at[0, d],
                self.s3.at[1, d],
                (self.dp, self.y * NZ + to),
            )
            copy.start()
            self.back_copies.append(copy)

    def arrived(self):
        for copy in self.back_copies:
            copy.wait_recv()

    def finish(self):
        for copy in self.copies + self.row_copies + self.back_copies:
            copy.wait_send()


def state_kernel(own_ref, co_ref, out_ref, *scratch):
    dp, seq, y, z = where_am_i()
    greet(z_peers(dp, y, z) + y_peers(dp, y, z))
    scan = Scan(own_ref, out_ref, co_ref, scratch, False)
    scan.start()
    scan.totals()
    scan.give_back()
    scan.arrived()
    scan.finish()


def softmax_pair_t(u):
    e1 = jnp.exp(u - jnp.max(u, 0, keepdims=True))
    e2 = jnp.exp(jnp.min(u, 0, keepdims=True) - u)
    p1 = e1 * (1.0 / jnp.sum(e1, 0, keepdims=True))
    p2 = e2 * (1.0 / jnp.sum(e2, 0, keepdims=True))
    return p1, p2


def middle_kernel(
    coef, spans_ref, q_ref, t_ref, v_ref, fk_ref, w_ref, st0_ref, st0z_ref, in_ref, inz_ref,
    gq_ref, back_ref, back1_ref, dfk_ref, f_s, x_s, p_s, m_s, both_s,
):
    head = pl.program_id(0)
    block = pl.program_id(1)
    seq = lax.axis_index("seq")
    starts = starts_of(spans_ref)
    b0 = 2 * seq
    in0 = no_start(starts, b0)
    same = no_start(starts, b0 + 1)
    in1 = no_start(starts, b0, b0 + 1)
    w_in = jnp.where(block == 0, in0, in1)
    w_st = jnp.where(block == 0, 0.0, same)
    top = lax.broadcasted_iota(jnp.int32, (16, 128), 0)
    m_s[0:128, :] = fk_ref[...]
    for half in (0, 1):
        rows = slice(half * 128, (half + 1) * 128)
        m_s[128:256, rows] = (w_in * in_ref[rows, :] + w_st * st0_ref[rows, :]).astype(BF16)
        zr = pl.ds(2 * head + half, 1)
        zb = w_in * inz_ref[zr, :] + w_st * st0z_ref[zr, :]
        m_s[256:272, rows] = jnp.where(top == 0, zb, 0.0).astype(BF16)
    v = v_ref[...]
    causal = lax.broadcasted_iota(jnp.int32, (SPAN, SPAN), 0) <= lax.broadcasted_iota(
        jnp.int32, (SPAN, SPAN), 1
    )
    for g in range(GROUP):
        cols = slice(g * HD, (g + 1) * HD)
        p1, p2 = softmax_pair_t(dot(w_ref[g], q_ref[:, cols], 0, 1))
        f_s[0:128, cols] = p1.astype(BF16)
        f_s[128:256, cols] = p2.astype(BF16)
        p_s[0, :, cols] = p1
        p_s[1, :, cols] = p2
    both_s[...] = dot(m_s[...], f_s[...], 1, 0)
    zcol = dot(m_s[256:272, :], jnp.ones((16, 128), BF16), 0, 0)
    invs = []
    for g in range(GROUP):
        cols = slice(g * HD, (g + 1) * HD)
        scores = jnp.where(causal, both_s[0:128, cols], 0.0)
        x_s[0:128, cols] = scores.astype(BF16)
        invs.append(1.0 / (jnp.sum(scores, 0, keepdims=True) + both_s[256:257, cols]))
    both_s[128:256, :] = both_s[128:256, :] + dot(v, x_s[0:128, :], 0, 0)
    eye = (
        lax.broadcasted_iota(jnp.int32, (HD, HD), 0) == lax.broadcasted_iota(jnp.int32, (HD, HD), 1)
    ).astype(F32).astype(BF16)
    ddens = []
    for g in range(GROUP):
        cols = slice(g * HD, (g + 1) * HD)
        inv = invs[g]
        out = both_s[128:256, cols] * inv
        dy = coef * (out - dot(eye, t_ref[:, cols], 1, 1))
        x_s[128:256, cols] = (dy * inv).astype(BF16)
        dden = -jnp.sum(dy * out, 0, keepdims=True) * inv
        ddens.append(dden)
        hi = dden.astype(BF16).astype(F32)
        mid = (dden - hi).astype(BF16).astype(F32)
        low = dden - hi - mid
        x_s[256:272, cols] = jnp.where(
            top == 0, hi, jnp.where(top == 1, mid, jnp.where(top == 2, low, 0.0))
        ).astype(BF16)
    both_s[0:128, :] = dot(v, x_s[128:256, :], 1, 0)
    for g in range(GROUP):
        cols = slice(g * HD, (g + 1) * HD)
        x_s[0:128, cols] = jnp.where(causal, both_s[0:128, cols] + ddens[g], 0.0).astype(BF16)
    both_s[0:256, :] = dot(m_s[0:256, :], x_s[0:256, :], 0, 0)
    for g in range(GROUP):
        cols = slice(g * HD, (g + 1) * HD)
        p1, p2 = p_s[0, :, cols], p_s[1, :, cols]
        d1 = both_s[0:128, cols] + zcol[0:128] * ddens[g]
        d2 = both_s[128:256, cols] + zcol[128:256] * ddens[g]
        s1 = jnp.sum(p1 * d1, 0, keepdims=True)
        s2 = jnp.sum(p2 * d2, 0, keepdims=True)
        duq = (p1 * (d1 - s1) - p2 * (d2 - s2)).astype(BF16)
        grad = dot(q_ref[:, cols], duq, 0, 1)
        gq_ref[g] = jnp.where(block == 0, 0.0, gq_ref[g]) + grad

    acc = dot(x_s[...], f_s[...], 1, 1)
    dfk_ref[...] = acc[0:128, :]

    @pl.when(jnp.logical_and(head == 0, block == 0))
    def _():
        back_ref[pl.ds(ZROW, ROWS - ZROW), :] = jnp.zeros((ROWS - ZROW, 128), F32)
        back1_ref[pl.ds(ZROW, ROWS - ZROW), :] = jnp.zeros((ROWS - ZROW, 128), F32)

    for half in (0, 1):
        lanes = slice(half * 128, (half + 1) * 128)
        part = acc[128:256, lanes]
        zpart = acc[256:257, lanes] + acc[257:258, lanes] + acc[258:259, lanes]
        rows = pl.ds(pl.multiple_of(head * 256 + half * 128, 128), 128)
        zr = pl.ds(ZROW + 2 * head + half, 1)

        @pl.when(block == 0)
        def _():
            back_ref[rows, :] = in0 * part
            back_ref[zr, :] = in0 * zpart

        @pl.when(block == 1)
        def _():
            back_ref[rows, :] = back_ref[rows, :] + in1 * part
            back_ref[zr, :] = back_ref[zr, :] + in1 * zpart
            back1_ref[rows, :] = part
            back1_ref[zr, :] = zpart


def send_all(items):
    copies = [remote(*item) for item in items]
    for copy in copies:
        copy.start()
    return copies


def last_kernel(
    spans_ref, own_ref, co_ref, back1_ref, dfk_ref, pk_ref, k_ref, v_ref, gq_ref,
    oq_ref, ok_ref, rin, half_in, half, xy_in, quarter, z_in, gk, kd_in, kd, ky_in, ky, kz_in,
    sc, sxy, sz, az, axy, ac, skd, sky, skz, aky, akd, *scratch,
):
    dp, seq, y, z = where_am_i()
    x, core = lax.div(dp, 2), lax.rem(dp, 2)

    def plane(d):
        px, py = lax.rem(x + d // 4, 4), lax.rem(y + d % 4, 4)
        return px, py, (px * 2 + core, py * NZ + z)

    mate = (x * 2 + (1 - core), seq)
    zs = z_peers(dp, y, z)
    dps = [(lax.rem(dp + d, NDP), seq) for d in range(1, NDP)]
    planes = [plane(d)[2] for d in range(1, 16)]
    other = [(lax.rem(x + d, 4) * 2 + (1 - core), seq) for d in range(4)]
    greet(zs + planes + other)

    scan = Scan(own_ref, rin, co_ref, scratch, True)
    scan.start()
    pair = send_all([(gq_ref.at[rows_of(1 - core, 2048)], half_in, sc.at[0], sc.at[1], mate)])
    pair[0].wait_recv()
    half[...] = gq_ref[rows_of(core, 2048), :] + half_in[...]
    spread = []
    for d in range(1, 16):
        px, py, dev = plane(d)
        spread.append((half.at[rows_of(px * 4 + py, 128)], xy_in.at[d], sxy.at[0, d], sxy.at[1, d], dev))
    spread = send_all(spread)
    scan.totals()
    scan.give_back()
    for copy in spread:
        copy.wait_recv()
    me_xy = x * 4 + y
    acc = half[rows_of(me_xy, 128), :]
    for d in range(1, 16):
        acc = acc + xy_in[d]
    quarter[...] = acc
    base = core * 2048 + me_xy * 128
    zsend = send_all([
        (quarter.at[rows_of(lax.rem(z + d, NZ), 16)], z_in.at[d], sz.at[0, d], sz.at[1, d], zs[d - 1])
        for d in range(1, NZ)
    ])
    scan.arrived()

    starts = starts_of(spans_ref)
    b0 = 2 * seq
    same = no_start(starts, b0 + 1)
    out0 = no_start(starts, b0 + 1, b0 + 2)
    out1 = no_start(starts, b0 + 2)
    for h in range(HK):
        cols = slice(h * HD, (h + 1) * HD)
        total = jnp.zeros((HD, HD), F32)
        for c in (0, 1):
            toks = slice(c * SPAN, (c + 1) * SPAN)
            grads = []
            for hf in (0, 1):
                rows = slice(h * 256 + hf * 128, h * 256 + (hf + 1) * 128)
                zr = slice(ZROW + 2 * h + hf, ZROW + 2 * h + hf + 1)
                if c == 0:
                    r = same * back1_ref[rows, :] + out0 * rin[rows, :]
                    rz = same * back1_ref[zr, :] + out0 * rin[zr, :]
                else:
                    r = out1 * rin[rows, :]
                    rz = out1 * rin[zr, :]
                f = slice(h * 256 + hf * 128, h * 256 + (hf + 1) * 128)
                grads.append(
                    dfk_ref[toks, f] + dot(v_ref[toks, cols], r.astype(BF16), 1, 0)
                    + rz.astype(BF16).astype(F32)
                )
            duk = map_grad(pk_ref[0, toks, cols], pk_ref[1, toks, cols], grads[0], grads[1])
            total = total + dot(k_ref[toks, cols], duk, 0, 0)
        gk[h * HD : (h + 1) * HD, :] = total
    kdsend = send_all([
        (gk.at[rows_of(lax.rem(dp + d, NDP), 64)], kd_in.at[d], skd.at[0, d], skd.at[1, d], dps[d - 1])
        for d in range(1, NDP)
    ])

    for copy in zsend:
        copy.wait_recv()
    acc = quarter[rows_of(z, 16), :]
    for d in range(1, NZ):
        acc = acc + z_in[d]
    mine = pl.ds(pl.multiple_of(base + z * 16, 8), 16)
    oq_ref[mine, :] = acc
    zback = send_all([
        (oq_ref.at[mine], oq_ref.at[mine], az.at[0, d], az.at[1, d], zs[d - 1]) for d in range(1, NZ)
    ])

    for copy in kdsend:
        copy.wait_recv()
    acc = gk[rows_of(dp, 64), :]
    for d in range(1, NDP):
        acc = acc + kd_in[d]
    kd[...] = acc
    ys = y_peers(dp, y, z)
    kysend = send_all([
        (kd.at[rows_of(lax.rem(y + d, NY), 16)], ky_in.at[d], sky.at[0, d], sky.at[1, d], ys[d - 1])
        for d in range(1, NY)
    ])

    for copy in zback:
        copy.wait_recv()
    block = pl.ds(pl.multiple_of(base, 128), 128)
    xyback = send_all([
        (oq_ref.at[block], oq_ref.at[block], axy.at[0, d], axy.at[1, d], planes[d - 1])
        for d in range(1, 16)
    ])

    for copy in kysend:
        copy.wait_recv()
    acc = kd[rows_of(y, 16), :]
    for d in range(1, NY):
        acc = acc + ky_in[d]
    ky[...] = acc
    kz_in[z] = acc
    kzsend = send_all([
        (ky, kz_in.at[z], skz.at[0, d], skz.at[1, d], zs[d - 1]) for d in range(1, NZ)
    ])
    for copy in kzsend:
        copy.wait_recv()
    acc = kz_in[0]
    for k in range(1, NZ):
        acc = acc + kz_in[k]
    kmine = pl.ds(pl.multiple_of(dp * 64 + y * 16, 8), 16)
    ok_ref[kmine, :] = acc
    kyback = send_all([
        (ok_ref.at[kmine], ok_ref.at[kmine], aky.at[0, d], aky.at[1, d], ys[d - 1]) for d in range(1, NY)
    ])
    for copy in kyback:
        copy.wait_recv()
    kblock = rows_of(dp, 64)
    kdback = send_all([
        (ok_ref.at[kblock], ok_ref.at[kblock], akd.at[0, d], akd.at[1, d], dps[d - 1])
        for d in range(1, NDP)
    ])

    for copy in xyback:
        copy.wait_recv()
    whole = rows_of(core, 2048)
    back = send_all([(oq_ref.at[whole], oq_ref.at[whole], ac.at[0], ac.at[1], mate)])
    for copy in kdback + back:
        copy.wait_recv()
    scan.finish()
    for copy in pair + spread + zsend + kdsend + zback + kysend + xyback + kzsend + kyback + kdback + back:
        copy.wait_send()


VM = pl.BlockSpec(memory_space=pltpu.VMEM)
SM = pl.BlockSpec(memory_space=pltpu.SMEM)
LIMIT = 56 * 1024 * 1024


def shape(dims, dtype=F32):
    return jax.ShapeDtypeStruct(dims, dtype)


def shards(queries, keys, values, targets, q_map, k_map, doc_spans):
    q, t = queries[0], targets[0]
    k, v = keys[0], values[0]
    toks = q.shape[0]
    coef = 2.0 / math.sqrt(lax.axis_size("dp") * lax.axis_size("seq") * toks * HD)
    fk, pk, st0, own, co = pl.pallas_call(
        key_kernel,
        out_shape=(
            shape((toks, HK * 256), BF16), shape((2, toks, HK * HD)), shape((ROWS, 128)),
            shape((ROWS, 128)), shape((16, 128)),
        ),
        in_specs=[SM, VM, VM, VM],
        out_specs=(VM,) * 5,
        compiler_params=pltpu.CompilerParams(vmem_limit_bytes=LIMIT),
        name="keys",
    )(doc_spans, k, v, k_map)

    state_in = pl.pallas_call(
        state_kernel,
        out_shape=shape((ROWS, 128)),
        in_specs=[VM, VM],
        out_specs=VM,
        scratch_shapes=scan_scratch(),
        compiler_params=pltpu.CompilerParams(
            collective_id=0, has_side_effects=True, vmem_limit_bytes=LIMIT
        ),
        name="scan",
    )(own, co)

    head_rows = pl.BlockSpec((256, 128), lambda i, c: (i, 0))
    z_rows = pl.BlockSpec((8, 128), lambda i, c: (ZROW // 8, 0))
    whole = pl.BlockSpec((ROWS, 128), lambda i, c: (0, 0))
    gq, back, back1, dfk = pl.pallas_call(
        functools.partial(middle_kernel, coef),
        grid=(HK, 2),
        out_shape=(
            shape((HK * GROUP, HD, HD)), shape((ROWS, 128)), shape((ROWS, 128)), shape((toks, HK * 256)),
        ),
        in_specs=[
            SM,
            pl.BlockSpec((SPAN, GROUP * HD), lambda i, c: (c, i)),
            pl.BlockSpec((SPAN, GROUP * HD), lambda i, c: (c, i)),
            pl.BlockSpec((SPAN, HD), lambda i, c: (c, i)),
            pl.BlockSpec((SPAN, 256), lambda i, c: (c, i)),
            pl.BlockSpec((GROUP, HD, HD), lambda i, c: (i, 0, 0)),
            head_rows, z_rows, head_rows, z_rows,
        ],
        out_specs=(
            pl.BlockSpec((GROUP, HD, HD), lambda i, c: (i, 0, 0)),
            whole, whole,
            pl.BlockSpec((SPAN, 256), lambda i, c: (c, i)),
        ),
        scratch_shapes=[
            pltpu.VMEM((256, GROUP * SPAN), BF16),
            pltpu.VMEM((272, GROUP * SPAN), BF16),
            pltpu.VMEM((2, 128, GROUP * SPAN), F32),
            pltpu.VMEM((272, 256), BF16),
            pltpu.VMEM((272, GROUP * SPAN), F32),
        ],
        compiler_params=pltpu.CompilerParams(
            dimension_semantics=("arbitrary", "arbitrary"), vmem_limit_bytes=LIMIT
        ),
        name="middle",
    )(doc_spans, q, t, v, fk, q_map, st0, st0, state_in, state_in)

    dma = pltpu.SemaphoreType.DMA
    gq, gk = pl.pallas_call(
        last_kernel,
        out_shape=(shape((HK * GROUP * HD, HD)), shape((HK * HD, HD))),
        in_specs=[SM] + [VM] * 8,
        out_specs=(VM, VM),
        scratch_shapes=[
            pltpu.VMEM((ROWS, 128), F32),
            pltpu.VMEM((2048, 128), F32),
            pltpu.VMEM((2048, 128), F32),
            pltpu.VMEM((16, 128, 128), F32),
            pltpu.VMEM((128, 128), F32),
            pltpu.VMEM((NZ, 16, 128), F32),
            pltpu.VMEM((HK * HD, 128), F32),
            pltpu.VMEM((NDP, 64, 128), F32),
            pltpu.VMEM((64, 128), F32),
            pltpu.VMEM((NY, 16, 128), F32),
            pltpu.VMEM((16, 128), F32),
            pltpu.VMEM((NZ, 16, 128), F32),
            dma((2,)), dma((2, 16)), dma((2, NZ)), dma((2, NZ)), dma((2, 16)), dma((2,)),
            dma((2, NDP)), dma((2, NY)), dma((2, NZ)), dma((2, NY)), dma((2, NDP)),
        ] + scan_scratch(),
        compiler_params=pltpu.CompilerParams(
            collective_id=1, has_side_effects=True, vmem_limit_bytes=LIMIT
        ),
        name="last",
    )(doc_spans, back, co, back1, dfk, pk, k, v, gq.reshape(HK * GROUP * HD, HD))
    return gq.reshape(HK * GROUP, HD, HD), gk.reshape(HK, HD, HD)


def solution(mesh):
    placed = (
        P("dp", "seq", None), P("dp", "seq", None), P("dp", "seq", None), P("dp", "seq", None),
        P(), P(), P("dp", None),
    )
    return jax.shard_map(shards, mesh=mesh, in_specs=placed, out_specs=(P(), P()), check_vma=False)
```

```python
import functools
import math

import jax
import jax.numpy as jnp
from jax import lax
from jax.experimental import pallas as pl
from jax.experimental.pallas import tpu as pltpu
from jax.sharding import PartitionSpec as P

MESH = pl.DeviceIdType.MESH
F32 = jnp.float32
BF16 = jnp.bfloat16
SPAN = 128
HD = 128
HK = 4
GROUP = 8
NDOC = 8
NZ = 8
NY = 4
NDP = 8
ZROW = 256
FIRST, LAST = 0, HK - 1


def dot(a, b, ca, cb):
    return lax.dot_general(a, b, (((ca,), (cb,)), ((), ())), preferred_element_type=F32)


def starts_of(spans_ref):
    starts, total = [], jnp.int32(0)
    for n in range(NDOC):
        starts.append(total)
        total = total + spans_ref[0, n]
    return starts


def no_start(starts, *blocks):
    hit = jnp.bool_(False)
    for s in starts:
        for b in blocks:
            hit = jnp.logical_or(hit, s == b)
    return jnp.where(hit, 0.0, 1.0).astype(F32)


def softmax_pair(u):
    e1 = jnp.exp(u - jnp.max(u, -1, keepdims=True))
    e2 = jnp.exp(jnp.min(u, -1, keepdims=True) - u)
    p1 = e1 * (1.0 / jnp.sum(e1, -1, keepdims=True))
    p2 = e2 * (1.0 / jnp.sum(e2, -1, keepdims=True))
    return p1, p2


def map_grad(p1, p2, d1, d2):
    s1 = jnp.sum(p1 * d1, -1, keepdims=True)
    s2 = jnp.sum(p2 * d2, -1, keepdims=True)
    return (p1 * (d1 - s1) - p2 * (d2 - s2)).astype(BF16)


def softmax_pair_t(u):
    e1 = jnp.exp(u - jnp.max(u, 0, keepdims=True))
    e2 = jnp.exp(jnp.min(u, 0, keepdims=True) - u)
    p1 = e1 * (1.0 / jnp.sum(e1, 0, keepdims=True))
    p2 = e2 * (1.0 / jnp.sum(e2, 0, keepdims=True))
    return p1, p2


def remote(src, dst, send, recv, dev):
    return pltpu.make_async_remote_copy(
        src_ref=src, dst_ref=dst, send_sem=send, recv_sem=recv, device_id=dev, device_id_type=MESH
    )


def send_all(items):
    copies = [remote(*item) for item in items]
    for copy in copies:
        copy.start()
    return copies


def rows_of(index, size):
    return pl.ds(pl.multiple_of(index * size, 8), size)


def slice_rows(head, holder):
    return 40 if head == holder else 32


def scan_scratch(holder):
    shapes = []
    for head in range(HK):
        size = slice_rows(head, holder)
        shapes += [
            pltpu.VMEM((NZ * size, 128), F32),
            pltpu.VMEM((NZ * size, 128), F32),
            pltpu.VMEM((NZ, size, 128), F32),
            pltpu.VMEM((size, 128), F32),
            pltpu.VMEM((2, size, 128), F32),
            pltpu.VMEM((NZ, size, 128), F32),
            pltpu.SemaphoreType.DMA((2, NZ)),
            pltpu.SemaphoreType.DMA((2, 2)),
            pltpu.SemaphoreType.DMA((2, NZ)),
        ]
    return shapes


class Scan:
    def __init__(self, at, co, scratch, size, reverse):
        self.co, self.size, self.reverse = co, size, reverse
        self.own, self.out, self.seen, self.total, self.rows_in, self.back = scratch[:6]
        self.s1, self.s2, self.s3 = scratch[6:]
        self.dp, self.seq, self.y, self.z = at
        self.order = list(range(NZ))[::-1] if reverse else list(range(NZ))

    def start(self):
        self.copies = send_all([
            (
                self.own.at[rows_of(lax.rem(self.z + d, NZ), self.size)], self.seen.at[self.z],
                self.s1.at[0, d], self.s1.at[1, d], (self.dp, self.y * NZ + lax.rem(self.z + d, NZ)),
            )
            for d in range(1, NZ)
        ])

    def totals(self):
        self.seen[self.z] = self.own[rows_of(self.z, self.size), :]
        for copy in self.copies:
            copy.wait_recv()
        acc = jnp.zeros((self.size, 128), F32)
        for k in self.order:
            self.back[k] = acc
            acc = self.seen[k] + self.co[k : k + 1, :] * acc
        self.total[...] = acc
        self.row_copies = send_all([
            (
                self.total, self.rows_in.at[d - 1], self.s2.at[0, d - 1], self.s2.at[1, d - 1],
                (self.dp, lax.rem(self.y + (NY - d if self.reverse else d), NY) * NZ + self.z),
            )
            for d in (1, 2)
        ])

    def give_back(self):
        for copy in self.row_copies:
            copy.wait_recv()
        first = 10 if self.reverse else 8
        carry = (
            self.co[first : first + 1, :] * self.rows_in[0]
            + self.co[first + 1 : first + 2, :] * self.rows_in[1]
        )
        keep = jnp.ones((1, 128), F32)
        for k in self.order:
            self.back[k] = self.back[k] + keep * carry
            keep = keep * self.co[k : k + 1, :]
        self.out[rows_of(self.z, self.size), :] = self.back[self.z]
        self.back_copies = send_all([
            (
                self.back.at[lax.rem(self.z + d, NZ)], self.out.at[rows_of(self.z, self.size)],
                self.s3.at[0, d], self.s3.at[1, d], (self.dp, self.y * NZ + lax.rem(self.z + d, NZ)),
            )
            for d in range(1, NZ)
        ])

    def arrived(self):
        for copy in self.back_copies:
            copy.wait_recv()

    def sent(self):
        return self.copies + self.row_copies + self.back_copies


def sum_scratch():
    dma = pltpu.SemaphoreType.DMA
    return [
        pltpu.VMEM((1024, 128), F32), pltpu.VMEM((1024, 128), F32), pltpu.VMEM((16, 64, 128), F32),
        pltpu.VMEM((64, 128), F32), pltpu.VMEM((NZ, 8, 128), F32),
        dma((2,)), dma((2, 16)), dma((2, NZ)), dma((2, NZ)), dma((2, 16)), dma((2,)),
    ]


class Total:
    def __init__(self, at, part, source, out, scratch, mate, planes, zs):
        self.source, self.out = source, out
        self.half_in, self.half, self.xy_in, self.quarter, self.z_in = scratch[:5]
        self.sc, self.sxy, self.sz, self.az, self.axy, self.ac = scratch[5:]
        self.mate, self.planes, self.zs = mate, planes, zs
        self.dp, self.seq, self.y, self.z = at
        self.x, self.core = lax.div(self.dp, 2), lax.rem(self.dp, 2)
        self.low = part * 2048
        self.base = self.low + self.core * 1024 + (self.x * 4 + self.y) * 64

    def core_rows(self, core):
        return pl.ds(pl.multiple_of(self.low + core * 1024, 8), 1024)

    def pair(self):
        self.c1 = send_all([
            (self.source.at[self.core_rows(1 - self.core)], self.half_in, self.sc.at[0], self.sc.at[1], self.mate)
        ])

    def plane(self):
        self.c1[0].wait_recv()
        self.half[...] = self.source[self.core_rows(self.core), :] + self.half_in[...]
        items = []
        for d in range(1, 16):
            spot = lax.rem(self.x + d // 4, 4) * 4 + lax.rem(self.y + d % 4, 4)
            items.append((
                self.half.at[rows_of(spot, 64)], self.xy_in.at[d], self.sxy.at[0, d], self.sxy.at[1, d],
                self.planes[d - 1],
            ))
        self.c2 = send_all(items)

    def along_z(self):
        for copy in self.c2:
            copy.wait_recv()
        acc = self.half[rows_of(self.x * 4 + self.y, 64), :]
        for d in range(1, 16):
            acc = acc + self.xy_in[d]
        self.quarter[...] = acc
        self.c3 = send_all([
            (
                self.quarter.at[rows_of(lax.rem(self.z + d, NZ), 8)], self.z_in.at[d],
                self.sz.at[0, d], self.sz.at[1, d], self.zs[d - 1],
            )
            for d in range(1, NZ)
        ])

    def back_z(self):
        for copy in self.c3:
            copy.wait_recv()
        acc = self.quarter[rows_of(self.z, 8), :]
        for d in range(1, NZ):
            acc = acc + self.z_in[d]
        mine = pl.ds(pl.multiple_of(self.base + self.z * 8, 8), 8)
        self.out[mine, :] = acc
        self.c4 = send_all([
            (self.out.at[mine], self.out.at[mine], self.az.at[0, d], self.az.at[1, d], self.zs[d - 1])
            for d in range(1, NZ)
        ])

    def back_plane(self):
        for copy in self.c4:
            copy.wait_recv()
        block = pl.ds(pl.multiple_of(self.base, 8), 64)
        self.c5 = send_all([
            (self.out.at[block], self.out.at[block], self.axy.at[0, d], self.axy.at[1, d], self.planes[d - 1])
            for d in range(1, 16)
        ])

    def back_pair(self):
        for copy in self.c5:
            copy.wait_recv()
        whole = self.core_rows(self.core)
        self.c6 = send_all([(self.out.at[whole], self.out.at[whole], self.ac.at[0], self.ac.at[1], self.mate)])

    def arrived(self):
        self.c6[0].wait_recv()

    def sent(self):
        return self.c1 + self.c2 + self.c3 + self.c4 + self.c5 + self.c6


N_SCAN = 9 * HK
N_SUM = 11


def whole_kernel(
    coef, spans_ref, q_hbm, k_ref, v_ref, t_hbm, w_hbm, wk_ref, oq_ref, ok_ref,
    q_s, t_s, w_s, fk_s, pk_s, st0_s, st0z_s, co_s, p_s, f_s, x_s, m_s, both_s, d_s, acc_s, gq_s,
    gk, kd_in, kd, ky_in, ky, kz_in, load, skd, sky, skz, aky, akd, *scratch,
):
    dp, seq = lax.axis_index("dp"), lax.axis_index("seq")
    y, z = lax.div(seq, NZ), lax.rem(seq, NZ)
    at = (dp, seq, y, z)
    x, core = lax.div(dp, 2), lax.rem(dp, 2)
    mate = (x * 2 + (1 - core), seq)
    zs = [(dp, y * NZ + lax.rem(z + d, NZ)) for d in range(1, NZ)]
    ys = [(dp, lax.rem(y + d, NY) * NZ + z) for d in range(1, NY)]
    dps = [(lax.rem(dp + d, NDP), seq) for d in range(1, NDP)]
    planes = [
        (lax.rem(x + d // 4, 4) * 2 + core, lax.rem(y + d % 4, 4) * NZ + z) for d in range(1, 16)
    ]
    other = [(lax.rem(x + d, 4) * 2 + (1 - core), seq) for d in range(4)]
    peers = zs + planes + other
    barrier = pltpu.get_barrier_semaphore()
    for dev in peers:
        pl.semaphore_signal(barrier, inc=1, device_id=dev, device_id_type=MESH)

    loads = []
    for h in range(HK):
        lanes = pl.ds(h * GROUP * HD, GROUP * HD)
        maps = pl.ds(h * GROUP, GROUP)
        loads.append([
            pltpu.make_async_copy(q_hbm.at[:, lanes], q_s.at[:, lanes], load.at[0, h]),
            pltpu.make_async_copy(w_hbm.at[maps], w_s.at[maps], load.at[1, h]),
            pltpu.make_async_copy(t_hbm.at[:, lanes], t_s.at[:, lanes], load.at[2, h]),
        ])
    for kind in range(3):
        for h in range(HK):
            loads[h][kind].start()

    starts = starts_of(spans_ref)
    b0 = 2 * seq
    in0 = no_start(starts, b0)
    same = no_start(starts, b0 + 1)
    in1 = no_start(starts, b0, b0 + 1)
    out0 = no_start(starts, b0 + 1, b0 + 2)
    out1 = no_start(starts, b0 + 2)
    halves = [(0, slice(0, 128)), (1, slice(128, 256))]

    fwd = [
        Scan(at, co_s, scratch[9 * h : 9 * h + 9], slice_rows(h, FIRST), False) for h in range(HK)
    ]
    rest = scratch[N_SCAN:]
    rev = [Scan(at, co_s, rest[9 * h : 9 * h + 9], slice_rows(h, LAST), True) for h in range(HK)]
    rest = rest[N_SCAN:]
    sums = [
        Total(at, p, gq_s, oq_ref, rest[N_SUM * p : N_SUM * p + N_SUM], mate, planes, zs) for p in (0, 1)
    ]

    fwd[FIRST].own[pl.ds(ZROW, 64), :] = jnp.zeros((64, 128), F32)
    rev[LAST].own[pl.ds(ZROW, 64), :] = jnp.zeros((64, 128), F32)
    for h in range(HK):
        cols = slice(h * HD, (h + 1) * HD)
        p1, p2 = softmax_pair(dot(k_ref[:, cols], wk_ref[h], 1, 0))
        pk_s[0, :, cols] = p1
        pk_s[1, :, cols] = p2
        fk = jnp.concatenate([p1, p2], -1).astype(BF16)
        fk_s[:, h * 256 : (h + 1) * 256] = fk
        v = v_ref[:, cols]
        toks = [slice(c * SPAN, (c + 1) * SPAN) for c in (0, 1)]
        st = [dot(v[r], fk[r], 0, 0) for r in toks]
        zsum = [jnp.sum(fk[r].astype(F32), 0, keepdims=True) for r in toks]
        for half, lanes in halves:
            rows = slice(half * 128, (half + 1) * 128)
            st0_s[h, rows, :] = st[0][:, lanes]
            fwd[h].own[rows, :] = same * st[0][:, lanes] + st[1][:, lanes]
            n = 2 * h + half
            st0z_s[n : n + 1, :] = zsum[0][:, lanes]
            fwd[FIRST].own[ZROW + n : ZROW + n + 1, :] = same * zsum[0][:, lanes] + zsum[1][:, lanes]
    pos = lax.broadcasted_iota(jnp.int32, (NZ, 128), 0) + y * NZ
    hit = jnp.zeros((NZ, 128), F32)
    before, after = jnp.float32(1.0), jnp.float32(1.0)
    for s in starts:
        hit = jnp.where(pos == s // 2, 1.0, hit)
        before = jnp.where(s // 16 == y - 1, 0.0, before)
        after = jnp.where(s // 16 == y + 1, 0.0, after)
    co_s[0:8, :] = 1.0 - hit
    co_s[8:9, :] = jnp.full((1, 128), jnp.where(y >= 1, 1.0, 0.0), F32)
    co_s[9:10, :] = jnp.full((1, 128), jnp.where(y >= 2, before, 0.0), F32)
    co_s[10:11, :] = jnp.full((1, 128), jnp.where(y <= 2, 1.0, 0.0), F32)
    co_s[11:12, :] = jnp.full((1, 128), jnp.where(y <= 1, after, 0.0), F32)

    pl.semaphore_wait(barrier, len(peers))
    for h in range(HK):
        fwd[h].start()

    def features(h):
        loads[h][0].wait()
        loads[h][1].wait()
        for g in range(GROUP):
            cols = slice((h * GROUP + g) * HD, (h * GROUP + g + 1) * HD)
            spot = slice(g * SPAN, (g + 1) * SPAN)
            p1, p2 = softmax_pair_t(dot(w_s[h * GROUP + g], q_s[:, cols], 0, 1))
            for c in (0, 1):
                toks = slice(c * SPAN, (c + 1) * SPAN)
                f_s[2 * h + c, 0:128, spot] = p1[:, toks].astype(BF16)
                f_s[2 * h + c, 128:256, spot] = p2[:, toks].astype(BF16)
                p_s[2 * h + c, 0, :, spot] = p1[:, toks]
                p_s[2 * h + c, 1, :, spot] = p2[:, toks]

    top = lax.broadcasted_iota(jnp.int32, (16, 128), 0)
    down = lax.broadcasted_iota(jnp.int32, (SPAN, SPAN), 0)
    across = lax.broadcasted_iota(jnp.int32, (SPAN, SPAN), 1)
    causal = down <= across
    eye = (down == across).astype(F32).astype(BF16)

    def middle(h):
        loads[h][2].wait()

        def one_block(c, carry):
            w_in = jnp.where(c == 0, in0, in1)
            w_st = jnp.where(c == 0, 0.0, same)
            toks = pl.ds(pl.multiple_of(c * SPAN, SPAN), SPAN)
            ic = 2 * h + c
            m_s[0:128, :] = fk_s[toks, h * 256 : (h + 1) * 256]
            for half, lanes in halves:
                rows = slice(half * 128, (half + 1) * 128)
                m_s[128:256, lanes] = (w_in * fwd[h].out[rows, :] + w_st * st0_s[h, rows, :]).astype(BF16)
                n = 2 * h + half
                zb = w_in * fwd[FIRST].out[ZROW + n : ZROW + n + 1, :] + w_st * st0z_s[n : n + 1, :]
                m_s[256:272, lanes] = jnp.where(top == 0, zb, 0.0).astype(BF16)
            v = v_ref[toks, h * HD : (h + 1) * HD]
            both_s[...] = dot(m_s[...], f_s[ic], 1, 0)
            zcol = dot(m_s[256:272, :], jnp.ones((16, 128), BF16), 0, 0)
            invs = []
            for g in range(GROUP):
                spot = slice(g * SPAN, (g + 1) * SPAN)
                scores = jnp.where(causal, both_s[0:128, spot], 0.0)
                x_s[0:128, spot] = scores.astype(BF16)
                invs.append(1.0 / (jnp.sum(scores, 0, keepdims=True) + both_s[256:257, spot]))
            both_s[128:256, :] = both_s[128:256, :] + dot(v, x_s[0:128, :], 0, 0)
            ddens = []
            for g in range(GROUP):
                cols = slice((h * GROUP + g) * HD, (h * GROUP + g + 1) * HD)
                spot = slice(g * SPAN, (g + 1) * SPAN)
                inv = invs[g]
                out = both_s[128:256, spot] * inv
                dy = coef * (out - dot(eye, t_s[toks, cols], 1, 1))
                x_s[128:256, spot] = (dy * inv).astype(BF16)
                dden = -jnp.sum(dy * out, 0, keepdims=True) * inv
                ddens.append(dden)
                hi = dden.astype(BF16).astype(F32)
                mid = (dden - hi).astype(BF16).astype(F32)
                low = dden - hi - mid
                x_s[256:272, spot] = jnp.where(
                    top == 0, hi, jnp.where(top == 1, mid, jnp.where(top == 2, low, 0.0))
                ).astype(BF16)
            both_s[0:128, :] = dot(v, x_s[128:256, :], 1, 0)
            for g in range(GROUP):
                spot = slice(g * SPAN, (g + 1) * SPAN)
                x_s[0:128, spot] = jnp.where(causal, both_s[0:128, spot] + ddens[g], 0.0).astype(BF16)
            both_s[0:256, :] = dot(m_s[0:256, :], x_s[0:256, :], 0, 0)
            for g in range(GROUP):
                spot = slice(g * SPAN, (g + 1) * SPAN)
                p1, p2 = p_s[ic, 0, :, spot], p_s[ic, 1, :, spot]
                d1 = both_s[0:128, spot] + zcol[0:128] * ddens[g]
                d2 = both_s[128:256, spot] + zcol[128:256] * ddens[g]
                s1 = jnp.sum(p1 * d1, 0, keepdims=True)
                s2 = jnp.sum(p2 * d2, 0, keepdims=True)
                d_s[c, :, spot] = (p1 * (d1 - s1) - p2 * (d2 - s2)).astype(BF16)
            acc_s[ic] = dot(x_s[...], f_s[ic], 1, 1)
            return carry

        lax.fori_loop(0, 2, one_block, 0)
        for g in range(GROUP):
            n = h * GROUP + g
            cols = slice(n * HD, (n + 1) * HD)
            spot = slice(g * SPAN, (g + 1) * SPAN)
            gq_s[n * HD : (n + 1) * HD, :] = dot(q_s[0:SPAN, cols], d_s[0, :, spot], 0, 1) + dot(
                q_s[SPAN : 2 * SPAN, cols], d_s[1, :, spot], 0, 1
            )
        for half, lanes in halves:
            rows = slice(half * 128, (half + 1) * 128)
            rev[h].own[rows, :] = in0 * acc_s[2 * h, 128:256, lanes] + in1 * acc_s[2 * h + 1, 128:256, lanes]
            gz = [sum_rows(acc_s, 2 * h + c, lanes) for c in (0, 1)]
            n = 2 * h + half
            rev[LAST].own[ZROW + n : ZROW + n + 1, :] = in0 * gz[0] + in1 * gz[1]

    a, b = sums
    features(0)
    features(1)
    fwd[0].totals()
    features(2)
    fwd[0].give_back()
    fwd[1].totals()
    features(3)
    fwd[1].give_back()
    fwd[2].totals()
    fwd[2].give_back()
    fwd[3].totals()
    fwd[3].give_back()

    fwd[0].arrived()
    middle(0)
    rev[0].start()
    fwd[1].arrived()
    middle(1)
    rev[1].start()
    a.pair()
    rev[0].totals()
    fwd[2].arrived()
    middle(2)
    rev[2].start()
    rev[0].give_back()
    rev[1].totals()
    a.plane()
    fwd[3].arrived()
    middle(3)
    rev[3].start()
    b.pair()
    rev[1].give_back()
    rev[2].totals()
    b.plane()
    a.along_z()
    rev[2].give_back()
    a.back_z()
    rev[3].totals()
    a.back_plane()
    b.along_z()
    rev[3].give_back()
    b.back_z()
    a.back_pair()
    for h in range(HK):
        rev[h].arrived()

    for h in range(HK):
        cols = slice(h * HD, (h + 1) * HD)
        total = jnp.zeros((HD, HD), F32)
        for c in (0, 1):
            toks = slice(c * SPAN, (c + 1) * SPAN)
            grads = []
            for half, lanes in halves:
                rows = slice(half * 128, (half + 1) * 128)
                zr = slice(ZROW + 2 * h + half, ZROW + 2 * h + half + 1)
                r, rz = rev[h].out[rows, :], rev[LAST].out[zr, :]
                if c == 0:
                    r = same * acc_s[2 * h + 1, 128:256, lanes] + out0 * r
                    rz = same * sum_rows(acc_s, 2 * h + 1, lanes) + out0 * rz
                else:
                    r, rz = out1 * r, out1 * rz
                grads.append(
                    acc_s[2 * h + c, 0:128, lanes] + dot(v_ref[toks, cols], r.astype(BF16), 1, 0)
                    + rz.astype(BF16).astype(F32)
                )
            duk = map_grad(pk_s[0, toks, cols], pk_s[1, toks, cols], grads[0], grads[1])
            total = total + dot(k_ref[toks, cols], duk, 0, 0)
        gk[cols, :] = total
    kdsend = send_all([
        (gk.at[rows_of(lax.rem(dp + d, NDP), 64)], kd_in.at[d], skd.at[0, d], skd.at[1, d], dps[d - 1])
        for d in range(1, NDP)
    ])
    b.back_plane()
    for copy in kdsend:
        copy.wait_recv()
    acc = gk[rows_of(dp, 64), :]
    for d in range(1, NDP):
        acc = acc + kd_in[d]
    kd[...] = acc
    kysend = send_all([
        (kd.at[rows_of(lax.rem(y + d, NY), 16)], ky_in.at[d], sky.at[0, d], sky.at[1, d], ys[d - 1])
        for d in range(1, NY)
    ])
    for copy in kysend:
        copy.wait_recv()
    acc = kd[rows_of(y, 16), :]
    for d in range(1, NY):
        acc = acc + ky_in[d]
    ky[...] = acc
    kz_in[z] = acc
    kzsend = send_all([
        (ky, kz_in.at[z], skz.at[0, d], skz.at[1, d], zs[d - 1]) for d in range(1, NZ)
    ])
    b.back_pair()
    for copy in kzsend:
        copy.wait_recv()
    acc = kz_in[0]
    for n in range(1, NZ):
        acc = acc + kz_in[n]
    kmine = pl.ds(pl.multiple_of(dp * 64 + y * 16, 8), 16)
    ok_ref[kmine, :] = acc
    kyback = send_all([
        (ok_ref.at[kmine], ok_ref.at[kmine], aky.at[0, d], aky.at[1, d], ys[d - 1]) for d in range(1, NY)
    ])
    for copy in kyback:
        copy.wait_recv()
    kblock = rows_of(dp, 64)
    kdback = send_all([
        (ok_ref.at[kblock], ok_ref.at[kblock], akd.at[0, d], akd.at[1, d], dps[d - 1])
        for d in range(1, NDP)
    ])
    a.arrived()
    b.arrived()
    for copy in kdback:
        copy.wait_recv()
    for part in fwd + rev + sums:
        for copy in part.sent():
            copy.wait_send()
    for copy in kdsend + kysend + kzsend + kyback + kdback:
        copy.wait_send()


def sum_rows(acc_s, index, lanes):
    return acc_s[index, 256:257, lanes] + acc_s[index, 257:258, lanes] + acc_s[index, 258:259, lanes]


VM = pl.BlockSpec(memory_space=pltpu.VMEM)
SM = pl.BlockSpec(memory_space=pltpu.SMEM)
ANY = pl.BlockSpec(memory_space=pl.ANY)
LIMIT = 60 * 1024 * 1024


def shards(queries, keys, values, targets, q_map, k_map, doc_spans):
    toks = queries.shape[1]
    heads = HK * GROUP
    coef = 2.0 / math.sqrt(lax.axis_size("dp") * lax.axis_size("seq") * toks * HD)
    dma = pltpu.SemaphoreType.DMA
    vmem = pltpu.VMEM
    gq, gk = pl.pallas_call(
        functools.partial(whole_kernel, coef),
        out_shape=(
            jax.ShapeDtypeStruct((heads * HD, HD), F32), jax.ShapeDtypeStruct((HK * HD, HD), F32),
        ),
        in_specs=[SM, ANY, VM, VM, ANY, ANY, VM],
        out_specs=(VM, VM),
        scratch_shapes=[
            vmem((toks, heads * HD), BF16),
            vmem((toks, heads * HD), BF16),
            vmem((heads, HD, HD), BF16),
            vmem((toks, HK * 256), BF16),
            vmem((2, toks, HK * HD), F32),
            vmem((HK, 256, 128), F32),
            vmem((8, 128), F32),
            vmem((16, 128), F32),
            vmem((2 * HK, 2, 128, GROUP * SPAN), F32),
            vmem((2 * HK, 256, GROUP * SPAN), BF16),
            vmem((272, GROUP * SPAN), BF16),
            vmem((272, 256), BF16),
            vmem((272, GROUP * SPAN), F32),
            vmem((2, HD, GROUP * SPAN), BF16),
            vmem((2 * HK, 272, 256), F32),
            vmem((heads * HD, HD), F32),
            vmem((HK * HD, HD), F32),
            vmem((NDP, 64, 128), F32),
            vmem((64, 128), F32),
            vmem((NY, 16, 128), F32),
            vmem((16, 128), F32),
            vmem((NZ, 16, 128), F32),
            dma((3, HK)),
            dma((2, NDP)), dma((2, NY)), dma((2, NZ)), dma((2, NY)), dma((2, NDP)),
        ] + scan_scratch(FIRST) + scan_scratch(LAST) + sum_scratch() + sum_scratch(),
        compiler_params=pltpu.CompilerParams(
            collective_id=0, has_side_effects=True, vmem_limit_bytes=LIMIT
        ),
        name="whole",
    )(doc_spans, queries[0], keys[0], values[0], targets[0], q_map, k_map)
    return gq.reshape(heads, HD, HD), gk.reshape(HK, HD, HD)


def solution(mesh):
    placed = (
        P("dp", "seq", None), P("dp", "seq", None), P("dp", "seq", None), P("dp", "seq", None),
        P(), P(), P("dp", None),
    )
    return jax.shard_map(shards, mesh=mesh, in_specs=placed, out_specs=(P(), P()), check_vma=False)
```

```python
import functools
import math

import jax
import jax.numpy as jnp
from jax import lax
from jax.experimental import pallas as pl
from jax.experimental.pallas import tpu as pltpu
from jax.sharding import PartitionSpec as P

MESH = pl.DeviceIdType.MESH
F32 = jnp.float32
BF16 = jnp.bfloat16
SPAN = 128
HD = 128
HK = 4
GROUP = 8
NDOC = 8
NZ = 8
NY = 4
NDP = 8
ZROW = 256
FIRST, LAST = 0, HK - 1


def dot(a, b, ca, cb):
    return lax.dot_general(a, b, (((ca,), (cb,)), ((), ())), preferred_element_type=F32)


def starts_of(spans_ref):
    starts, total = [], jnp.int32(0)
    for n in range(NDOC):
        starts.append(total)
        total = total + spans_ref[0, n]
    return starts


def no_start(starts, *blocks):
    hit = jnp.bool_(False)
    for s in starts:
        for b in blocks:
            hit = jnp.logical_or(hit, s == b)
    return jnp.where(hit, 0.0, 1.0).astype(F32)


def softmax_pair(u):
    e1 = jnp.exp(u - jnp.max(u, -1, keepdims=True))
    e2 = jnp.exp(jnp.min(u, -1, keepdims=True) - u)
    p1 = e1 * (1.0 / jnp.sum(e1, -1, keepdims=True))
    p2 = e2 * (1.0 / jnp.sum(e2, -1, keepdims=True))
    return p1, p2


def map_grad(p1, p2, d1, d2):
    s1 = jnp.sum(p1 * d1, -1, keepdims=True)
    s2 = jnp.sum(p2 * d2, -1, keepdims=True)
    return (p1 * (d1 - s1) - p2 * (d2 - s2)).astype(BF16)


def softmax_pair_t(u):
    e1 = jnp.exp(u - jnp.max(u, 0, keepdims=True))
    e2 = jnp.exp(jnp.min(u, 0, keepdims=True) - u)
    p1 = e1 * (1.0 / jnp.sum(e1, 0, keepdims=True))
    p2 = e2 * (1.0 / jnp.sum(e2, 0, keepdims=True))
    return p1, p2


def remote(src, dst, send, recv, dev):
    return pltpu.make_async_remote_copy(
        src_ref=src, dst_ref=dst, send_sem=send, recv_sem=recv, device_id=dev, device_id_type=MESH
    )


def send_all(items):
    copies = [remote(*item) for item in items]
    for copy in copies:
        copy.start()
    return copies


def rows_of(index, size):
    return pl.ds(pl.multiple_of(index * size, 8), size)


def slice_rows(head, holder):
    return 40 if head == holder else 32


def scan_scratch(holder):
    shapes = []
    for head in range(HK):
        size = slice_rows(head, holder)
        shapes += [
            pltpu.VMEM((NZ * size, 128), F32),
            pltpu.VMEM((NZ * size, 128), F32),
            pltpu.VMEM((NZ, size, 128), F32),
            pltpu.VMEM((size, 128), F32),
            pltpu.VMEM((2, size, 128), F32),
            pltpu.VMEM((NZ, size, 128), F32),
            pltpu.SemaphoreType.DMA((2, NZ)),
            pltpu.SemaphoreType.DMA((2, 2)),
            pltpu.SemaphoreType.DMA((2, NZ)),
        ]
    return shapes


class Scan:
    def __init__(self, at, co, scratch, size, reverse):
        self.co, self.size, self.reverse = co, size, reverse
        self.own, self.out, self.seen, self.total, self.rows_in, self.back = scratch[:6]
        self.s1, self.s2, self.s3 = scratch[6:]
        self.dp, self.seq, self.y, self.z = at
        self.order = list(range(NZ))[::-1] if reverse else list(range(NZ))

    def start(self):
        self.copies = send_all([
            (
                self.own.at[rows_of(lax.rem(self.z + d, NZ), self.size)], self.seen.at[self.z],
                self.s1.at[0, d], self.s1.at[1, d], (self.dp, self.y * NZ + lax.rem(self.z + d, NZ)),
            )
            for d in range(1, NZ)
        ])

    def totals(self):
        self.seen[self.z] = self.own[rows_of(self.z, self.size), :]
        for copy in self.copies:
            copy.wait_recv()
        acc = jnp.zeros((self.size, 128), F32)
        for k in self.order:
            self.back[k] = acc
            acc = self.seen[k] + self.co[k : k + 1, :] * acc
        self.total[...] = acc
        self.row_copies = send_all([
            (
                self.total, self.rows_in.at[d - 1], self.s2.at[0, d - 1], self.s2.at[1, d - 1],
                (self.dp, lax.rem(self.y + (NY - d if self.reverse else d), NY) * NZ + self.z),
            )
            for d in (1, 2)
        ])

    def give_back(self):
        for copy in self.row_copies:
            copy.wait_recv()
        first = 10 if self.reverse else 8
        carry = (
            self.co[first : first + 1, :] * self.rows_in[0]
            + self.co[first + 1 : first + 2, :] * self.rows_in[1]
        )
        keep = jnp.ones((1, 128), F32)
        for k in self.order:
            self.back[k] = self.back[k] + keep * carry
            keep = keep * self.co[k : k + 1, :]
        self.out[rows_of(self.z, self.size), :] = self.back[self.z]
        self.back_copies = send_all([
            (
                self.back.at[lax.rem(self.z + d, NZ)], self.out.at[rows_of(self.z, self.size)],
                self.s3.at[0, d], self.s3.at[1, d], (self.dp, self.y * NZ + lax.rem(self.z + d, NZ)),
            )
            for d in range(1, NZ)
        ])

    def arrived(self):
        for copy in self.back_copies:
            copy.wait_recv()

    def sent(self):
        return self.copies + self.row_copies + self.back_copies


def sum_scratch():
    dma = pltpu.SemaphoreType.DMA
    return [
        pltpu.VMEM((1024, 128), F32), pltpu.VMEM((1024, 128), F32), pltpu.VMEM((16, 64, 128), F32),
        pltpu.VMEM((64, 128), F32), pltpu.VMEM((NZ, 8, 128), F32),
        dma((2,)), dma((2, 16)), dma((2, NZ)), dma((2, NZ)), dma((2, 16)), dma((2,)),
    ]


class Total:
    def __init__(self, at, part, source, out, scratch, mate, planes, zs):
        self.source, self.out = source, out
        self.half_in, self.half, self.xy_in, self.quarter, self.z_in = scratch[:5]
        self.sc, self.sxy, self.sz, self.az, self.axy, self.ac = scratch[5:]
        self.mate, self.planes, self.zs = mate, planes, zs
        self.dp, self.seq, self.y, self.z = at
        self.x, self.core = lax.div(self.dp, 2), lax.rem(self.dp, 2)
        self.low = part * 2048
        self.base = self.low + self.core * 1024 + (self.x * 4 + self.y) * 64

    def core_rows(self, core):
        return pl.ds(pl.multiple_of(self.low + core * 1024, 8), 1024)

    def pair(self):
        self.c1 = send_all([
            (self.source.at[self.core_rows(1 - self.core)], self.half_in, self.sc.at[0], self.sc.at[1], self.mate)
        ])

    def plane(self):
        self.c1[0].wait_recv()
        self.half[...] = self.source[self.core_rows(self.core), :] + self.half_in[...]
        items = []
        for d in range(1, 16):
            spot = lax.rem(self.x + d // 4, 4) * 4 + lax.rem(self.y + d % 4, 4)
            items.append((
                self.half.at[rows_of(spot, 64)], self.xy_in.at[d], self.sxy.at[0, d], self.sxy.at[1, d],
                self.planes[d - 1],
            ))
        self.c2 = send_all(items)

    def along_z(self):
        for copy in self.c2:
            copy.wait_recv()
        acc = self.half[rows_of(self.x * 4 + self.y, 64), :]
        for d in range(1, 16):
            acc = acc + self.xy_in[d]
        self.quarter[...] = acc
        self.c3 = send_all([
            (
                self.quarter.at[rows_of(lax.rem(self.z + d, NZ), 8)], self.z_in.at[d],
                self.sz.at[0, d], self.sz.at[1, d], self.zs[d - 1],
            )
            for d in range(1, NZ)
        ])

    def back_z(self):
        for copy in self.c3:
            copy.wait_recv()
        acc = self.quarter[rows_of(self.z, 8), :]
        for d in range(1, NZ):
            acc = acc + self.z_in[d]
        mine = pl.ds(pl.multiple_of(self.base + self.z * 8, 8), 8)
        self.out[mine, :] = acc
        self.c4 = send_all([
            (self.out.at[mine], self.out.at[mine], self.az.at[0, d], self.az.at[1, d], self.zs[d - 1])
            for d in range(1, NZ)
        ])

    def back_plane(self):
        for copy in self.c4:
            copy.wait_recv()
        block = pl.ds(pl.multiple_of(self.base, 8), 64)
        self.c5 = send_all([
            (self.out.at[block], self.out.at[block], self.axy.at[0, d], self.axy.at[1, d], self.planes[d - 1])
            for d in range(1, 16)
        ])

    def back_pair(self):
        for copy in self.c5:
            copy.wait_recv()
        whole = self.core_rows(self.core)
        self.c6 = send_all([(self.out.at[whole], self.out.at[whole], self.ac.at[0], self.ac.at[1], self.mate)])

    def arrived(self):
        self.c6[0].wait_recv()

    def sent(self):
        return self.c1 + self.c2 + self.c3 + self.c4 + self.c5 + self.c6


N_SCAN = 9 * HK
N_SUM = 11


def whole_kernel(
    coef, spans_ref, q_hbm, k_ref, v_ref, t_hbm, w_hbm, wk_ref, oq_ref, ok_ref,
    q_s, t_s, w_s, fk_s, pk_s, st0_s, st0z_s, co_s, p_s, f_s, x_s, m_s, both_s, d_s, acc_s, gq_s, den_s, num_s,
    gk, kd_in, ky, kz_in, load, skd, skz, akd, *scratch,
):
    dp, seq = lax.axis_index("dp"), lax.axis_index("seq")
    y, z = lax.div(seq, NZ), lax.rem(seq, NZ)
    at = (dp, seq, y, z)
    x, core = lax.div(dp, 2), lax.rem(dp, 2)
    mate = (x * 2 + (1 - core), seq)
    zs = [(dp, y * NZ + lax.rem(z + d, NZ)) for d in range(1, NZ)]
    planes = [
        (lax.rem(x + d // 4, 4) * 2 + core, lax.rem(y + d % 4, 4) * NZ + z) for d in range(1, 16)
    ]
    layer = [
        (lax.rem(dp + d // NY, NDP), lax.rem(y + d % NY, NY) * NZ + z) for d in range(1, NDP * NY)
    ]
    peers = zs + layer
    barrier = pltpu.get_barrier_semaphore()
    for dev in peers:
        pl.semaphore_signal(barrier, inc=1, device_id=dev, device_id_type=MESH)

    loads = []
    for h in range(HK):
        lanes = pl.ds(h * GROUP * HD, GROUP * HD)
        maps = pl.ds(h * GROUP, GROUP)
        loads.append([
            pltpu.make_async_copy(q_hbm.at[:, lanes], q_s.at[:, lanes], load.at[0, h]),
            pltpu.make_async_copy(w_hbm.at[maps], w_s.at[maps], load.at[1, h]),
            pltpu.make_async_copy(t_hbm.at[:, lanes], t_s.at[:, lanes], load.at[2, h]),
        ])
    for kind in range(3):
        for h in range(HK):
            loads[h][kind].start()

    starts = starts_of(spans_ref)
    b0 = 2 * seq
    in0 = no_start(starts, b0)
    same = no_start(starts, b0 + 1)
    in1 = no_start(starts, b0, b0 + 1)
    out0 = no_start(starts, b0 + 1, b0 + 2)
    out1 = no_start(starts, b0 + 2)
    halves = [(0, slice(0, 128)), (1, slice(128, 256))]

    fwd = [
        Scan(at, co_s, scratch[9 * h : 9 * h + 9], slice_rows(h, FIRST), False) for h in range(HK)
    ]
    rest = scratch[N_SCAN:]
    rev = [Scan(at, co_s, rest[9 * h : 9 * h + 9], slice_rows(h, LAST), True) for h in range(HK)]
    rest = rest[N_SCAN:]
    sums = [
        Total(at, p, gq_s, oq_ref, rest[N_SUM * p : N_SUM * p + N_SUM], mate, planes, zs) for p in (0, 1)
    ]

    fwd[FIRST].own[pl.ds(ZROW, 64), :] = jnp.zeros((64, 128), F32)
    rev[LAST].own[pl.ds(ZROW, 64), :] = jnp.zeros((64, 128), F32)
    for h in range(HK):
        cols = slice(h * HD, (h + 1) * HD)
        p1, p2 = softmax_pair(dot(k_ref[:, cols], wk_ref[h], 1, 0))
        pk_s[0, :, cols] = p1
        pk_s[1, :, cols] = p2
        fk = jnp.concatenate([p1, p2], -1).astype(BF16)
        fk_s[:, h * 256 : (h + 1) * 256] = fk
        v = v_ref[:, cols]
        toks = [slice(c * SPAN, (c + 1) * SPAN) for c in (0, 1)]
        st = [dot(v[r], fk[r], 0, 0) for r in toks]
        zsum = [jnp.sum(fk[r].astype(F32), 0, keepdims=True) for r in toks]
        for half, lanes in halves:
            rows = slice(half * 128, (half + 1) * 128)
            st0_s[h, rows, :] = st[0][:, lanes]
            fwd[h].own[rows, :] = same * st[0][:, lanes] + st[1][:, lanes]
            n = 2 * h + half
            st0z_s[n : n + 1, :] = zsum[0][:, lanes]
            fwd[FIRST].own[ZROW + n : ZROW + n + 1, :] = same * zsum[0][:, lanes] + zsum[1][:, lanes]
    pos = lax.broadcasted_iota(jnp.int32, (NZ, 128), 0) + y * NZ
    hit = jnp.zeros((NZ, 128), F32)
    before, after = jnp.float32(1.0), jnp.float32(1.0)
    for s in starts:
        hit = jnp.where(pos == s // 2, 1.0, hit)
        before = jnp.where(s // 16 == y - 1, 0.0, before)
        after = jnp.where(s // 16 == y + 1, 0.0, after)
    co_s[0:8, :] = 1.0 - hit
    co_s[8:9, :] = jnp.full((1, 128), jnp.where(y >= 1, 1.0, 0.0), F32)
    co_s[9:10, :] = jnp.full((1, 128), jnp.where(y >= 2, before, 0.0), F32)
    co_s[10:11, :] = jnp.full((1, 128), jnp.where(y <= 2, 1.0, 0.0), F32)
    co_s[11:12, :] = jnp.full((1, 128), jnp.where(y <= 1, after, 0.0), F32)

    pl.semaphore_wait(barrier, len(peers))
    for h in range(HK):
        fwd[h].start()

    def features(h):
        loads[h][0].wait()
        loads[h][1].wait()
        for g in range(GROUP):
            cols = slice((h * GROUP + g) * HD, (h * GROUP + g + 1) * HD)
            spot = slice(g * SPAN, (g + 1) * SPAN)
            p1, p2 = softmax_pair_t(dot(w_s[h * GROUP + g], q_s[:, cols], 0, 1))
            for c in (0, 1):
                toks = slice(c * SPAN, (c + 1) * SPAN)
                f_s[2 * h + c, 0:128, spot] = p1[:, toks].astype(BF16)
                f_s[2 * h + c, 128:256, spot] = p2[:, toks].astype(BF16)
                p_s[2 * h + c, 0, :, spot] = p1[:, toks]
                p_s[2 * h + c, 1, :, spot] = p2[:, toks]

    top = lax.broadcasted_iota(jnp.int32, (16, 128), 0)
    down = lax.broadcasted_iota(jnp.int32, (SPAN, SPAN), 0)
    across = lax.broadcasted_iota(jnp.int32, (SPAN, SPAN), 1)
    causal = down <= across
    eye = (down == across).astype(F32).astype(BF16)

    def local(h):
        def one_block(c, carry):
            toks = pl.ds(pl.multiple_of(c * SPAN, SPAN), SPAN)
            ic = 2 * h + c
            both_s[0:128, :] = dot(fk_s[toks, h * 256 : (h + 1) * 256], f_s[ic], 1, 0)
            for g in range(GROUP):
                spot = slice(g * SPAN, (g + 1) * SPAN)
                scores = jnp.where(causal, both_s[0:128, spot], 0.0)
                x_s[0:128, spot] = scores.astype(BF16)
                den_s[ic, 0:1, spot] = jnp.sum(scores, 0, keepdims=True)
            num_s[ic] = dot(v_ref[toks, h * HD : (h + 1) * HD], x_s[0:128, :], 0, 0)
            return carry

        lax.fori_loop(0, 2, one_block, 0)

    def middle(h):
        loads[h][2].wait()

        def one_block(c, carry):
            w_in = jnp.where(c == 0, in0, in1)
            w_st = jnp.where(c == 0, 0.0, same)
            toks = pl.ds(pl.multiple_of(c * SPAN, SPAN), SPAN)
            ic = 2 * h + c
            m_s[0:128, :] = fk_s[toks, h * 256 : (h + 1) * 256]
            for half, lanes in halves:
                rows = slice(half * 128, (half + 1) * 128)
                m_s[128:256, lanes] = (w_in * fwd[h].out[rows, :] + w_st * st0_s[h, rows, :]).astype(BF16)
                n = 2 * h + half
                zb = w_in * fwd[FIRST].out[ZROW + n : ZROW + n + 1, :] + w_st * st0z_s[n : n + 1, :]
                m_s[256:272, lanes] = jnp.where(top == 0, zb, 0.0).astype(BF16)
            v = v_ref[toks, h * HD : (h + 1) * HD]
            both_s[128:272, :] = dot(m_s[128:272, :], f_s[ic], 1, 0)
            zcol = dot(m_s[256:272, :], jnp.ones((16, 128), BF16), 0, 0)
            ddens = []
            for g in range(GROUP):
                cols = slice((h * GROUP + g) * HD, (h * GROUP + g + 1) * HD)
                spot = slice(g * SPAN, (g + 1) * SPAN)
                inv = 1.0 / (den_s[ic, 0:1, spot] + both_s[256:257, spot])
                out = (num_s[ic, :, spot] + both_s[128:256, spot]) * inv
                dy = coef * (out - dot(eye, t_s[toks, cols], 1, 1))
                x_s[128:256, spot] = (dy * inv).astype(BF16)
                dden = -jnp.sum(dy * out, 0, keepdims=True) * inv
                ddens.append(dden)
                hi = dden.astype(BF16).astype(F32)
                mid = (dden - hi).astype(BF16).astype(F32)
                low = dden - hi - mid
                x_s[256:272, spot] = jnp.where(
                    top == 0, hi, jnp.where(top == 1, mid, jnp.where(top == 2, low, 0.0))
                ).astype(BF16)
            both_s[0:128, :] = dot(v, x_s[128:256, :], 1, 0)
            for g in range(GROUP):
                spot = slice(g * SPAN, (g + 1) * SPAN)
                x_s[0:128, spot] = jnp.where(causal, both_s[0:128, spot] + ddens[g], 0.0).astype(BF16)
            both_s[0:256, :] = dot(m_s[0:256, :], x_s[0:256, :], 0, 0)
            for g in range(GROUP):
                spot = slice(g * SPAN, (g + 1) * SPAN)
                p1, p2 = p_s[ic, 0, :, spot], p_s[ic, 1, :, spot]
                d1 = both_s[0:128, spot] + zcol[0:128] * ddens[g]
                d2 = both_s[128:256, spot] + zcol[128:256] * ddens[g]
                s1 = jnp.sum(p1 * d1, 0, keepdims=True)
                s2 = jnp.sum(p2 * d2, 0, keepdims=True)
                d_s[c, :, spot] = (p1 * (d1 - s1) - p2 * (d2 - s2)).astype(BF16)
            acc_s[ic] = dot(x_s[...], f_s[ic], 1, 1)
            return carry

        lax.fori_loop(0, 2, one_block, 0)
        for g in range(GROUP):
            n = h * GROUP + g
            cols = slice(n * HD, (n + 1) * HD)
            spot = slice(g * SPAN, (g + 1) * SPAN)
            gq_s[n * HD : (n + 1) * HD, :] = dot(q_s[0:SPAN, cols], d_s[0, :, spot], 0, 1) + dot(
                q_s[SPAN : 2 * SPAN, cols], d_s[1, :, spot], 0, 1
            )
        for half, lanes in halves:
            rows = slice(half * 128, (half + 1) * 128)
            rev[h].own[rows, :] = in0 * acc_s[2 * h, 128:256, lanes] + in1 * acc_s[2 * h + 1, 128:256, lanes]
            gz = [sum_rows(acc_s, 2 * h + c, lanes) for c in (0, 1)]
            n = 2 * h + half
            rev[LAST].own[ZROW + n : ZROW + n + 1, :] = in0 * gz[0] + in1 * gz[1]

    a, b = sums
    features(0)
    features(1)
    fwd[0].totals()
    features(2)
    local(0)
    fwd[0].give_back()
    fwd[1].totals()
    features(3)
    fwd[1].give_back()
    fwd[2].totals()
    local(1)
    fwd[3].totals()
    fwd[2].give_back()
    local(2)
    fwd[3].give_back()
    local(3)
    fwd[0].arrived()
    middle(0)
    rev[0].start()
    fwd[1].arrived()
    middle(1)
    rev[1].start()
    a.pair()
    fwd[2].arrived()
    a.plane()
    middle(2)
    rev[2].start()
    rev[0].totals()
    fwd[3].arrived()
    middle(3)
    rev[3].start()
    b.pair()
    rev[1].totals()
    rev[0].give_back()
    b.plane()
    rev[2].totals()
    rev[1].give_back()
    a.along_z()
    rev[2].give_back()
    a.back_z()
    rev[3].totals()
    a.back_plane()
    b.along_z()
    rev[3].give_back()
    b.back_z()
    for h in range(HK):
        rev[h].arrived()

    for h in range(HK):
        cols = slice(h * HD, (h + 1) * HD)
        total = jnp.zeros((HD, HD), F32)
        for c in (0, 1):
            toks = slice(c * SPAN, (c + 1) * SPAN)
            grads = []
            for half, lanes in halves:
                rows = slice(half * 128, (half + 1) * 128)
                zr = slice(ZROW + 2 * h + half, ZROW + 2 * h + half + 1)
                r, rz = rev[h].out[rows, :], rev[LAST].out[zr, :]
                if c == 0:
                    r = same * acc_s[2 * h + 1, 128:256, lanes] + out0 * r
                    rz = same * sum_rows(acc_s, 2 * h + 1, lanes) + out0 * rz
                else:
                    r, rz = out1 * r, out1 * rz
                grads.append(
                    acc_s[2 * h + c, 0:128, lanes] + dot(v_ref[toks, cols], r.astype(BF16), 1, 0)
                    + rz.astype(BF16).astype(F32)
                )
            duk = map_grad(pk_s[0, toks, cols], pk_s[1, toks, cols], grads[0], grads[1])
            total = total + dot(k_ref[toks, cols], duk, 0, 0)
        gk[cols, :] = total
    kdsend = send_all([
        (
            gk.at[rows_of(lax.rem(dp + d // NY, NDP) * NY + lax.rem(y + d % NY, NY), 16)], kd_in.at[d],
            skd.at[0, d], skd.at[1, d], layer[d - 1],
        )
        for d in range(1, NDP * NY)
    ])
    a.back_pair()
    for copy in kdsend:
        copy.wait_recv()
    acc = gk[rows_of(dp * NY + y, 16), :]
    for d in range(1, NDP * NY):
        acc = acc + kd_in[d]
    ky[...] = acc
    kz_in[z] = acc
    kzsend = send_all([
        (ky, kz_in.at[z], skz.at[0, d], skz.at[1, d], zs[d - 1]) for d in range(1, NZ)
    ])
    b.back_plane()
    for copy in kzsend:
        copy.wait_recv()
    acc = kz_in[0]
    for n in range(1, NZ):
        acc = acc + kz_in[n]
    kmine = rows_of(dp * NY + y, 16)
    ok_ref[kmine, :] = acc
    kdback = send_all([
        (ok_ref.at[kmine], ok_ref.at[kmine], akd.at[0, d], akd.at[1, d], layer[d - 1])
        for d in range(1, NDP * NY)
    ])
    b.back_pair()
    a.arrived()
    b.arrived()
    for copy in kdback:
        copy.wait_recv()
    for part in fwd + rev + sums:
        for copy in part.sent():
            copy.wait_send()
    for copy in kdsend + kzsend + kdback:
        copy.wait_send()


def sum_rows(acc_s, index, lanes):
    return acc_s[index, 256:257, lanes] + acc_s[index, 257:258, lanes] + acc_s[index, 258:259, lanes]


VM = pl.BlockSpec(memory_space=pltpu.VMEM)
SM = pl.BlockSpec(memory_space=pltpu.SMEM)
ANY = pl.BlockSpec(memory_space=pl.ANY)
LIMIT = 51200 * 1024


def shards(queries, keys, values, targets, q_map, k_map, doc_spans):
    toks = queries.shape[1]
    heads = HK * GROUP
    coef = 2.0 / math.sqrt(lax.axis_size("dp") * lax.axis_size("seq") * toks * HD)
    dma = pltpu.SemaphoreType.DMA
    vmem = pltpu.VMEM
    gq, gk = pl.pallas_call(
        functools.partial(whole_kernel, coef),
        out_shape=(
            jax.ShapeDtypeStruct((heads * HD, HD), F32), jax.ShapeDtypeStruct((HK * HD, HD), F32),
        ),
        in_specs=[SM, ANY, VM, VM, ANY, ANY, VM],
        out_specs=(VM, VM),
        scratch_shapes=[
            vmem((toks, heads * HD), BF16),
            vmem((toks, heads * HD), BF16),
            vmem((heads, HD, HD), BF16),
            vmem((toks, HK * 256), BF16),
            vmem((2, toks, HK * HD), F32),
            vmem((HK, 256, 128), F32),
            vmem((8, 128), F32),
            vmem((16, 128), F32),
            vmem((2 * HK, 2, 128, GROUP * SPAN), F32),
            vmem((2 * HK, 256, GROUP * SPAN), BF16),
            vmem((272, GROUP * SPAN), BF16),
            vmem((272, 256), BF16),
            vmem((272, GROUP * SPAN), F32),
            vmem((2, HD, GROUP * SPAN), BF16),
            vmem((2 * HK, 272, 256), F32),
            vmem((heads * HD, HD), F32),
            vmem((2 * HK, 8, GROUP * SPAN), F32),
            vmem((2 * HK, HD, GROUP * SPAN), F32),
            vmem((HK * HD, HD), F32),
            vmem((NDP * NY, 16, 128), F32),
            vmem((16, 128), F32),
            vmem((NZ, 16, 128), F32),
            dma((3, HK)),
            dma((2, NDP * NY)), dma((2, NZ)), dma((2, NDP * NY)),
        ] + scan_scratch(FIRST) + scan_scratch(LAST) + sum_scratch() + sum_scratch(),
        compiler_params=pltpu.CompilerParams(
            collective_id=0, has_side_effects=True, vmem_limit_bytes=LIMIT
        ),
        name="whole",
    )(doc_spans, queries[0], keys[0], values[0], targets[0], q_map, k_map)
    return gq.reshape(heads, HD, HD), gk.reshape(HK, HD, HD)


def solution(mesh):
    placed = (
        P("dp", "seq", None), P("dp", "seq", None), P("dp", "seq", None), P("dp", "seq", None),
        P(), P(), P("dp", None),
    )
    return jax.shard_map(shards, mesh=mesh, in_specs=placed, out_specs=(P(), P()), check_vma=False)
```

```python
import functools
import math

import jax
import jax.numpy as jnp
from jax import lax
from jax.experimental import pallas as pl
from jax.experimental.pallas import tpu as pltpu
from jax.sharding import PartitionSpec as P

MESH = pl.DeviceIdType.MESH
F32 = jnp.float32
BF16 = jnp.bfloat16
SPAN = 128
HD = 128
HK = 4
GROUP = 8
NDOC = 8
NZ = 8
NY = 4
NDP = 8
ZROW = 256
FIRST, LAST = 0, HK - 1


def dot(a, b, ca, cb):
    return lax.dot_general(a, b, (((ca,), (cb,)), ((), ())), preferred_element_type=F32)


def starts_of(spans_ref):
    starts, total = [], jnp.int32(0)
    for n in range(NDOC):
        starts.append(total)
        total = total + spans_ref[0, n]
    return starts


def no_start(starts, *blocks):
    hit = jnp.bool_(False)
    for s in starts:
        for b in blocks:
            hit = jnp.logical_or(hit, s == b)
    return jnp.where(hit, 0.0, 1.0).astype(F32)


def softmax_pair(u):
    e1 = jnp.exp(u - jnp.max(u, -1, keepdims=True))
    e2 = jnp.exp(jnp.min(u, -1, keepdims=True) - u)
    p1 = e1 * (1.0 / jnp.sum(e1, -1, keepdims=True))
    p2 = e2 * (1.0 / jnp.sum(e2, -1, keepdims=True))
    return p1, p2


def map_grad(p1, p2, d1, d2):
    s1 = jnp.sum(p1 * d1, -1, keepdims=True)
    s2 = jnp.sum(p2 * d2, -1, keepdims=True)
    return (p1 * (d1 - s1) - p2 * (d2 - s2)).astype(BF16)


def softmax_pair_t(u):
    e1 = jnp.exp(u - jnp.max(u, 0, keepdims=True))
    e2 = jnp.exp(jnp.min(u, 0, keepdims=True) - u)
    p1 = e1 * (1.0 / jnp.sum(e1, 0, keepdims=True))
    p2 = e2 * (1.0 / jnp.sum(e2, 0, keepdims=True))
    return p1, p2


def remote(src, dst, send, recv, dev):
    return pltpu.make_async_remote_copy(
        src_ref=src, dst_ref=dst, send_sem=send, recv_sem=recv, device_id=dev, device_id_type=MESH
    )


def send_all(items):
    copies = [remote(*item) for item in items]
    for copy in copies:
        copy.start()
    return copies


def rows_of(index, size):
    return pl.ds(pl.multiple_of(index * size, 8), size)


def slice_rows(head, holder):
    return 40 if head == holder else 32


def scan_scratch(holder):
    shapes = []
    for head in range(HK):
        size = slice_rows(head, holder)
        shapes += [
            pltpu.VMEM((NZ * size, 128), F32),
            pltpu.VMEM((NZ * size, 128), F32),
            pltpu.VMEM((NZ, size, 128), F32),
            pltpu.VMEM((size, 128), F32),
            pltpu.VMEM((2, size, 128), F32),
            pltpu.VMEM((NZ, size, 128), F32),
            pltpu.SemaphoreType.DMA((2, NZ)),
            pltpu.SemaphoreType.DMA((2, 2)),
            pltpu.SemaphoreType.DMA((2, NZ)),
        ]
    return shapes


class Scan:
    def __init__(self, at, co, scratch, size, reverse):
        self.co, self.size, self.reverse = co, size, reverse
        self.own, self.out, self.seen, self.total, self.rows_in, self.back = scratch[:6]
        self.s1, self.s2, self.s3 = scratch[6:]
        self.dp, self.seq, self.y, self.z = at
        self.order = list(range(NZ))[::-1] if reverse else list(range(NZ))

    def start(self):
        self.copies = send_all([
            (
                self.own.at[rows_of(lax.rem(self.z + d, NZ), self.size)], self.seen.at[self.z],
                self.s1.at[0, d], self.s1.at[1, d], (self.dp, self.y * NZ + lax.rem(self.z + d, NZ)),
            )
            for d in range(1, NZ)
        ])

    def totals(self):
        self.seen[self.z] = self.own[rows_of(self.z, self.size), :]
        for copy in self.copies:
            copy.wait_recv()
        acc = jnp.zeros((self.size, 128), F32)
        for k in self.order:
            self.back[k] = acc
            acc = self.seen[k] + self.co[k : k + 1, :] * acc
        self.total[...] = acc
        self.row_copies = send_all([
            (
                self.total, self.rows_in.at[d - 1], self.s2.at[0, d - 1], self.s2.at[1, d - 1],
                (self.dp, lax.rem(self.y + (NY - d if self.reverse else d), NY) * NZ + self.z),
            )
            for d in (1, 2)
        ])

    def give_back(self):
        for copy in self.row_copies:
            copy.wait_recv()
        first = 10 if self.reverse else 8
        carry = (
            self.co[first : first + 1, :] * self.rows_in[0]
            + self.co[first + 1 : first + 2, :] * self.rows_in[1]
        )
        keep = jnp.ones((1, 128), F32)
        for k in self.order:
            self.back[k] = self.back[k] + keep * carry
            keep = keep * self.co[k : k + 1, :]
        self.out[rows_of(self.z, self.size), :] = self.back[self.z]
        self.back_copies = send_all([
            (
                self.back.at[lax.rem(self.z + d, NZ)], self.out.at[rows_of(self.z, self.size)],
                self.s3.at[0, d], self.s3.at[1, d], (self.dp, self.y * NZ + lax.rem(self.z + d, NZ)),
            )
            for d in range(1, NZ)
        ])

    def arrived(self):
        for copy in self.back_copies:
            copy.wait_recv()

    def sent(self):
        return self.copies + self.row_copies + self.back_copies


def sum_scratch():
    dma = pltpu.SemaphoreType.DMA
    return [
        pltpu.VMEM((1024, 128), F32), pltpu.VMEM((1024, 128), F32), pltpu.VMEM((16, 64, 128), F32),
        pltpu.VMEM((64, 128), F32), pltpu.VMEM((NZ, 8, 128), F32),
        dma((2,)), dma((2, 16)), dma((2, NZ)), dma((2, NZ)), dma((2, 16)), dma((2,)),
    ]


class Total:
    def __init__(self, at, part, source, out, scratch, mate, planes, zs):
        self.source, self.out = source, out
        self.half_in, self.half, self.xy_in, self.quarter, self.z_in = scratch[:5]
        self.sc, self.sxy, self.sz, self.az, self.axy, self.ac = scratch[5:]
        self.mate, self.planes, self.zs = mate, planes, zs
        self.dp, self.seq, self.y, self.z = at
        self.x, self.core = lax.div(self.dp, 2), lax.rem(self.dp, 2)
        self.low = part * 2048
        self.base = self.low + self.core * 1024 + (self.x * 4 + self.y) * 64

    def core_rows(self, core):
        return pl.ds(pl.multiple_of(self.low + core * 1024, 8), 1024)

    def pair(self):
        self.c1 = send_all([
            (self.source.at[self.core_rows(1 - self.core)], self.half_in, self.sc.at[0], self.sc.at[1], self.mate)
        ])

    def plane(self):
        self.c1[0].wait_recv()
        self.half[...] = self.source[self.core_rows(self.core), :] + self.half_in[...]
        items = []
        for d in range(1, 16):
            spot = lax.rem(self.x + d // 4, 4) * 4 + lax.rem(self.y + d % 4, 4)
            items.append((
                self.half.at[rows_of(spot, 64)], self.xy_in.at[d], self.sxy.at[0, d], self.sxy.at[1, d],
                self.planes[d - 1],
            ))
        self.c2 = send_all(items)

    def along_z(self):
        for copy in self.c2:
            copy.wait_recv()
        acc = self.half[rows_of(self.x * 4 + self.y, 64), :]
        for d in range(1, 16):
            acc = acc + self.xy_in[d]
        self.quarter[...] = acc
        self.c3 = send_all([
            (
                self.quarter.at[rows_of(lax.rem(self.z + d, NZ), 8)], self.z_in.at[d],
                self.sz.at[0, d], self.sz.at[1, d], self.zs[d - 1],
            )
            for d in range(1, NZ)
        ])

    def back_z(self):
        for copy in self.c3:
            copy.wait_recv()
        acc = self.quarter[rows_of(self.z, 8), :]
        for d in range(1, NZ):
            acc = acc + self.z_in[d]
        mine = pl.ds(pl.multiple_of(self.base + self.z * 8, 8), 8)
        self.out[mine, :] = acc
        self.c4 = send_all([
            (self.out.at[mine], self.out.at[mine], self.az.at[0, d], self.az.at[1, d], self.zs[d - 1])
            for d in range(1, NZ)
        ])

    def back_plane(self):
        for copy in self.c4:
            copy.wait_recv()
        block = pl.ds(pl.multiple_of(self.base, 8), 64)
        self.c5 = send_all([
            (self.out.at[block], self.out.at[block], self.axy.at[0, d], self.axy.at[1, d], self.planes[d - 1])
            for d in range(1, 16)
        ])

    def back_pair(self):
        for copy in self.c5:
            copy.wait_recv()
        whole = self.core_rows(self.core)
        self.c6 = send_all([(self.out.at[whole], self.out.at[whole], self.ac.at[0], self.ac.at[1], self.mate)])

    def arrived(self):
        self.c6[0].wait_recv()

    def sent(self):
        return self.c1 + self.c2 + self.c3 + self.c4 + self.c5 + self.c6


N_SCAN = 9 * HK
N_SUM = 11


def whole_kernel(
    coef, spans_ref, q_hbm, k_ref, v_ref, t_hbm, w_hbm, wk_ref, oq_ref, ok_ref,
    q_s, t_s, w_s, fk_s, pk_s, st0_s, st0z_s, co_s, p_s, f_s, x_s, m_s, both_s, d_s, acc_s, gq_s, den_s, num_s,
    gk, kd_in, ky, kz_in, load, skd, skz, akd, *scratch,
):
    dp, seq = lax.axis_index("dp"), lax.axis_index("seq")
    y, z = lax.div(seq, NZ), lax.rem(seq, NZ)
    at = (dp, seq, y, z)
    x, core = lax.div(dp, 2), lax.rem(dp, 2)
    mate = (x * 2 + (1 - core), seq)
    zs = [(dp, y * NZ + lax.rem(z + d, NZ)) for d in range(1, NZ)]
    planes = [
        (lax.rem(x + d // 4, 4) * 2 + core, lax.rem(y + d % 4, 4) * NZ + z) for d in range(1, 16)
    ]
    layer = [
        (lax.rem(dp + d // NY, NDP), lax.rem(y + d % NY, NY) * NZ + z) for d in range(1, NDP * NY)
    ]
    peers = zs + layer
    barrier = pltpu.get_barrier_semaphore()
    for dev in peers:
        pl.semaphore_signal(barrier, inc=1, device_id=dev, device_id_type=MESH)

    loads = []
    for h in range(HK):
        lanes = pl.ds(h * GROUP * HD, GROUP * HD)
        maps = pl.ds(h * GROUP, GROUP)
        loads.append([
            pltpu.make_async_copy(q_hbm.at[:, lanes], q_s.at[:, lanes], load.at[0, h]),
            pltpu.make_async_copy(w_hbm.at[maps], w_s.at[maps], load.at[1, h]),
            pltpu.make_async_copy(t_hbm.at[:, lanes], t_s.at[:, lanes], load.at[2, h]),
        ])
    for kind in range(3):
        for h in range(HK):
            loads[h][kind].start()

    starts = starts_of(spans_ref)
    b0 = 2 * seq
    in0 = no_start(starts, b0)
    same = no_start(starts, b0 + 1)
    in1 = no_start(starts, b0, b0 + 1)
    out0 = no_start(starts, b0 + 1, b0 + 2)
    out1 = no_start(starts, b0 + 2)
    halves = [(0, slice(0, 128)), (1, slice(128, 256))]

    fwd = [
        Scan(at, co_s, scratch[9 * h : 9 * h + 9], slice_rows(h, FIRST), False) for h in range(HK)
    ]
    rest = scratch[N_SCAN:]
    rev = [Scan(at, co_s, rest[9 * h : 9 * h + 9], slice_rows(h, LAST), True) for h in range(HK)]
    rest = rest[N_SCAN:]
    sums = [
        Total(at, p, gq_s, oq_ref, rest[N_SUM * p : N_SUM * p + N_SUM], mate, planes, zs) for p in (0, 1)
    ]

    fwd[FIRST].own[pl.ds(ZROW, 64), :] = jnp.zeros((64, 128), F32)
    rev[LAST].own[pl.ds(ZROW, 64), :] = jnp.zeros((64, 128), F32)
    for h in range(HK):
        cols = slice(h * HD, (h + 1) * HD)
        p1, p2 = softmax_pair(dot(k_ref[:, cols], wk_ref[h], 1, 0))
        pk_s[0, :, cols] = p1
        pk_s[1, :, cols] = p2
        fk = jnp.concatenate([p1, p2], -1).astype(BF16)
        fk_s[:, h * 256 : (h + 1) * 256] = fk
        v = v_ref[:, cols]
        toks = [slice(c * SPAN, (c + 1) * SPAN) for c in (0, 1)]
        st = [dot(v[r], fk[r], 0, 0) for r in toks]
        zsum = [jnp.sum(fk[r].astype(F32), 0, keepdims=True) for r in toks]
        for half, lanes in halves:
            rows = slice(half * 128, (half + 1) * 128)
            st0_s[h, rows, :] = st[0][:, lanes]
            fwd[h].own[rows, :] = same * st[0][:, lanes] + st[1][:, lanes]
            n = 2 * h + half
            st0z_s[n : n + 1, :] = zsum[0][:, lanes]
            fwd[FIRST].own[ZROW + n : ZROW + n + 1, :] = same * zsum[0][:, lanes] + zsum[1][:, lanes]
    pos = lax.broadcasted_iota(jnp.int32, (NZ, 128), 0) + y * NZ
    hit = jnp.zeros((NZ, 128), F32)
    before, after = jnp.float32(1.0), jnp.float32(1.0)
    for s in starts:
        hit = jnp.where(pos == s // 2, 1.0, hit)
        before = jnp.where(s // 16 == y - 1, 0.0, before)
        after = jnp.where(s // 16 == y + 1, 0.0, after)
    co_s[0:8, :] = 1.0 - hit
    co_s[8:9, :] = jnp.full((1, 128), jnp.where(y >= 1, 1.0, 0.0), F32)
    co_s[9:10, :] = jnp.full((1, 128), jnp.where(y >= 2, before, 0.0), F32)
    co_s[10:11, :] = jnp.full((1, 128), jnp.where(y <= 2, 1.0, 0.0), F32)
    co_s[11:12, :] = jnp.full((1, 128), jnp.where(y <= 1, after, 0.0), F32)

    pl.semaphore_wait(barrier, len(peers))
    for h in range(HK):
        fwd[h].start()

    def features(h):
        loads[h][0].wait()
        loads[h][1].wait()
        for g in range(GROUP):
            cols = slice((h * GROUP + g) * HD, (h * GROUP + g + 1) * HD)
            spot = slice(g * SPAN, (g + 1) * SPAN)
            p1, p2 = softmax_pair_t(dot(w_s[h * GROUP + g], q_s[:, cols], 0, 1))
            for c in (0, 1):
                toks = slice(c * SPAN, (c + 1) * SPAN)
                f_s[2 * h + c, 0:128, spot] = p1[:, toks].astype(BF16)
                f_s[2 * h + c, 128:256, spot] = p2[:, toks].astype(BF16)
                p_s[2 * h + c, 0, :, spot] = p1[:, toks]
                p_s[2 * h + c, 1, :, spot] = p2[:, toks]

    top = lax.broadcasted_iota(jnp.int32, (16, 128), 0)
    down = lax.broadcasted_iota(jnp.int32, (SPAN, SPAN), 0)
    across = lax.broadcasted_iota(jnp.int32, (SPAN, SPAN), 1)
    causal = down <= across
    eye = (down == across).astype(F32).astype(BF16)

    def local(h):
        def one_block(c, carry):
            toks = pl.ds(pl.multiple_of(c * SPAN, SPAN), SPAN)
            ic = 2 * h + c
            both_s[0:128, :] = dot(fk_s[toks, h * 256 : (h + 1) * 256], f_s[ic], 1, 0)
            for g in range(GROUP):
                spot = slice(g * SPAN, (g + 1) * SPAN)
                scores = jnp.where(causal, both_s[0:128, spot], 0.0)
                x_s[0:128, spot] = scores.astype(BF16)
                den_s[ic, 0:1, spot] = jnp.sum(scores, 0, keepdims=True)
            num_s[ic] = dot(v_ref[toks, h * HD : (h + 1) * HD], x_s[0:128, :], 0, 0)
            return carry

        lax.fori_loop(0, 2, one_block, 0)

    def middle(h):
        loads[h][2].wait()

        def one_block(c, carry):
            w_in = jnp.where(c == 0, in0, in1)
            w_st = jnp.where(c == 0, 0.0, same)
            toks = pl.ds(pl.multiple_of(c * SPAN, SPAN), SPAN)
            ic = 2 * h + c
            m_s[0:128, :] = fk_s[toks, h * 256 : (h + 1) * 256]
            for half, lanes in halves:
                rows = slice(half * 128, (half + 1) * 128)
                m_s[128:256, lanes] = (w_in * fwd[h].out[rows, :] + w_st * st0_s[h, rows, :]).astype(BF16)
                n = 2 * h + half
                zb = w_in * fwd[FIRST].out[ZROW + n : ZROW + n + 1, :] + w_st * st0z_s[n : n + 1, :]
                m_s[256:272, lanes] = jnp.where(top == 0, zb, 0.0).astype(BF16)
            v = v_ref[toks, h * HD : (h + 1) * HD]
            both_s[128:272, :] = dot(m_s[128:272, :], f_s[ic], 1, 0)
            zcol = dot(m_s[256:272, :], jnp.ones((16, 128), BF16), 0, 0)
            ddens = []
            for g in range(GROUP):
                cols = slice((h * GROUP + g) * HD, (h * GROUP + g + 1) * HD)
                spot = slice(g * SPAN, (g + 1) * SPAN)
                inv = 1.0 / (den_s[ic, 0:1, spot] + both_s[256:257, spot])
                out = (num_s[ic, :, spot] + both_s[128:256, spot]) * inv
                dy = coef * (out - dot(eye, t_s[toks, cols], 1, 1))
                x_s[128:256, spot] = (dy * inv).astype(BF16)
                dden = -jnp.sum(dy * out, 0, keepdims=True) * inv
                ddens.append(dden)
                hi = dden.astype(BF16).astype(F32)
                mid = (dden - hi).astype(BF16).astype(F32)
                low = dden - hi - mid
                x_s[256:272, spot] = jnp.where(
                    top == 0, hi, jnp.where(top == 1, mid, jnp.where(top == 2, low, 0.0))
                ).astype(BF16)
            both_s[0:128, :] = dot(v, x_s[128:256, :], 1, 0)
            for g in range(GROUP):
                spot = slice(g * SPAN, (g + 1) * SPAN)
                x_s[0:128, spot] = jnp.where(causal, both_s[0:128, spot] + ddens[g], 0.0).astype(BF16)
            both_s[0:256, :] = dot(m_s[0:256, :], x_s[0:256, :], 0, 0)
            for g in range(GROUP):
                spot = slice(g * SPAN, (g + 1) * SPAN)
                p1, p2 = p_s[ic, 0, :, spot], p_s[ic, 1, :, spot]
                d1 = both_s[0:128, spot] + zcol[0:128] * ddens[g]
                d2 = both_s[128:256, spot] + zcol[128:256] * ddens[g]
                s1 = jnp.sum(p1 * d1, 0, keepdims=True)
                s2 = jnp.sum(p2 * d2, 0, keepdims=True)
                d_s[c, :, spot] = (p1 * (d1 - s1) - p2 * (d2 - s2)).astype(BF16)
            acc_s[ic] = dot(x_s[...], f_s[ic], 1, 1)
            return carry

        lax.fori_loop(0, 2, one_block, 0)
        for g in range(GROUP):
            n = h * GROUP + g
            cols = slice(n * HD, (n + 1) * HD)
            spot = slice(g * SPAN, (g + 1) * SPAN)
            gq_s[n * HD : (n + 1) * HD, :] = dot(q_s[0:SPAN, cols], d_s[0, :, spot], 0, 1) + dot(
                q_s[SPAN : 2 * SPAN, cols], d_s[1, :, spot], 0, 1
            )
        for half, lanes in halves:
            rows = slice(half * 128, (half + 1) * 128)
            rev[h].own[rows, :] = in0 * acc_s[2 * h, 128:256, lanes] + in1 * acc_s[2 * h + 1, 128:256, lanes]
            gz = [sum_rows(acc_s, 2 * h + c, lanes) for c in (0, 1)]
            n = 2 * h + half
            rev[LAST].own[ZROW + n : ZROW + n + 1, :] = in0 * gz[0] + in1 * gz[1]

    a, b = sums
    features(0)
    features(1)
    features(2)
    local(0)
    fwd[0].totals()
    features(3)
    fwd[1].totals()
    fwd[0].give_back()
    local(1)
    fwd[2].totals()
    fwd[1].give_back()
    local(2)
    fwd[3].totals()
    fwd[2].give_back()
    local(3)
    fwd[3].give_back()
    fwd[0].arrived()
    middle(0)
    rev[0].start()
    fwd[1].arrived()
    middle(1)
    rev[1].start()
    a.pair()
    fwd[2].arrived()
    a.plane()
    middle(2)
    rev[2].start()
    rev[0].totals()
    fwd[3].arrived()
    middle(3)
    rev[3].start()
    b.pair()
    a.along_z()
    rev[1].totals()
    rev[0].give_back()
    b.plane()
    rev[2].totals()
    rev[1].give_back()
    rev[2].give_back()
    rev[3].totals()
    a.back_z()
    b.along_z()
    rev[3].give_back()
    a.back_plane()
    b.back_z()
    for h in range(HK):
        rev[h].arrived()

    for h in range(HK):
        cols = slice(h * HD, (h + 1) * HD)
        total = jnp.zeros((HD, HD), F32)
        for c in (0, 1):
            toks = slice(c * SPAN, (c + 1) * SPAN)
            grads = []
            for half, lanes in halves:
                rows = slice(half * 128, (half + 1) * 128)
                zr = slice(ZROW + 2 * h + half, ZROW + 2 * h + half + 1)
                r, rz = rev[h].out[rows, :], rev[LAST].out[zr, :]
                if c == 0:
                    r = same * acc_s[2 * h + 1, 128:256, lanes] + out0 * r
                    rz = same * sum_rows(acc_s, 2 * h + 1, lanes) + out0 * rz
                else:
                    r, rz = out1 * r, out1 * rz
                grads.append(
                    acc_s[2 * h + c, 0:128, lanes] + dot(v_ref[toks, cols], r.astype(BF16), 1, 0)
                    + rz.astype(BF16).astype(F32)
                )
            duk = map_grad(pk_s[0, toks, cols], pk_s[1, toks, cols], grads[0], grads[1])
            total = total + dot(k_ref[toks, cols], duk, 0, 0)
        gk[cols, :] = total
    kdsend = send_all([
        (
            gk.at[rows_of(lax.rem(dp + d // NY, NDP) * NY + lax.rem(y + d % NY, NY), 16)], kd_in.at[d],
            skd.at[0, d], skd.at[1, d], layer[d - 1],
        )
        for d in range(1, NDP * NY)
    ])
    a.back_pair()
    for copy in kdsend:
        copy.wait_recv()
    acc = gk[rows_of(dp * NY + y, 16), :]
    for d in range(1, NDP * NY):
        acc = acc + kd_in[d]
    ky[...] = acc
    kz_in[z] = acc
    kzsend = send_all([
        (ky, kz_in.at[z], skz.at[0, d], skz.at[1, d], zs[d - 1]) for d in range(1, NZ)
    ])
    b.back_plane()
    for copy in kzsend:
        copy.wait_recv()
    acc = kz_in[0]
    for n in range(1, NZ):
        acc = acc + kz_in[n]
    kmine = rows_of(dp * NY + y, 16)
    ok_ref[kmine, :] = acc
    kdback = send_all([
        (ok_ref.at[kmine], ok_ref.at[kmine], akd.at[0, d], akd.at[1, d], layer[d - 1])
        for d in range(1, NDP * NY)
    ])
    b.back_pair()
    a.arrived()
    b.arrived()
    for copy in kdback:
        copy.wait_recv()
    for part in fwd + rev + sums:
        for copy in part.sent():
            copy.wait_send()
    for copy in kdsend + kzsend + kdback:
        copy.wait_send()


def sum_rows(acc_s, index, lanes):
    return acc_s[index, 256:257, lanes] + acc_s[index, 257:258, lanes] + acc_s[index, 258:259, lanes]


OUT_PARTS = 8


def store_kernel(a_ref, b_ref, oa_ref, ob_ref, a_s, b_s, sems):
    part = a_s.shape[0] // OUT_PARTS
    pieces = [(a_ref, a_s, oa_ref, pl.ds(n * part, part)) for n in range(OUT_PARTS)]
    pieces.append((b_ref, b_s, ob_ref, pl.ds(0, b_s.shape[0])))
    into = [
        pltpu.make_async_copy(src.at[r], held.at[r], sems.at[0, n])
        for n, (src, held, _, r) in enumerate(pieces)
    ]
    out = [
        pltpu.make_async_copy(held.at[r], dst.at[r], sems.at[1, n])
        for n, (_, held, dst, r) in enumerate(pieces)
    ]
    for copy in into:
        copy.start()
    for n in range(len(pieces)):
        into[n].wait()
        out[n].start()
    for copy in out:
        copy.wait()


VM = pl.BlockSpec(memory_space=pltpu.VMEM)
SM = pl.BlockSpec(memory_space=pltpu.SMEM)
ANY = pl.BlockSpec(memory_space=pl.ANY)
LIMIT = 60 * 1024 * 1024


def shards(queries, keys, values, targets, q_map, k_map, doc_spans):
    toks = queries.shape[1]
    heads = HK * GROUP
    coef = 2.0 / math.sqrt(lax.axis_size("dp") * lax.axis_size("seq") * toks * HD)
    dma = pltpu.SemaphoreType.DMA
    vmem = pltpu.VMEM
    gq, gk = pl.pallas_call(
        functools.partial(whole_kernel, coef),
        out_shape=(
            jax.ShapeDtypeStruct((heads * HD, HD), F32), jax.ShapeDtypeStruct((HK * HD, HD), F32),
        ),
        in_specs=[SM, ANY, VM, VM, ANY, ANY, VM],
        out_specs=(VM, VM),
        scratch_shapes=[
            vmem((toks, heads * HD), BF16),
            vmem((toks, heads * HD), BF16),
            vmem((heads, HD, HD), BF16),
            vmem((toks, HK * 256), BF16),
            vmem((2, toks, HK * HD), F32),
            vmem((HK, 256, 128), F32),
            vmem((8, 128), F32),
            vmem((16, 128), F32),
            vmem((2 * HK, 2, 128, GROUP * SPAN), F32),
            vmem((2 * HK, 256, GROUP * SPAN), BF16),
            vmem((272, GROUP * SPAN), BF16),
            vmem((272, 256), BF16),
            vmem((272, GROUP * SPAN), F32),
            vmem((2, HD, GROUP * SPAN), BF16),
            vmem((2 * HK, 272, 256), F32),
            vmem((heads * HD, HD), F32),
            vmem((2 * HK, 8, GROUP * SPAN), F32),
            vmem((2 * HK, HD, GROUP * SPAN), F32),
            vmem((HK * HD, HD), F32),
            vmem((NDP * NY, 16, 128), F32),
            vmem((16, 128), F32),
            vmem((NZ, 16, 128), F32),
            dma((3, HK)),
            dma((2, NDP * NY)), dma((2, NZ)), dma((2, NDP * NY)),
        ] + scan_scratch(FIRST) + scan_scratch(LAST) + sum_scratch() + sum_scratch(),
        compiler_params=pltpu.CompilerParams(
            collective_id=0, has_side_effects=True, vmem_limit_bytes=LIMIT
        ),
        name="whole",
    )(doc_spans, queries[0], keys[0], values[0], targets[0], q_map, k_map)
    gq, gk = pl.pallas_call(
        store_kernel,
        out_shape=(
            jax.ShapeDtypeStruct((heads, HD, HD), F32), jax.ShapeDtypeStruct((HK, HD, HD), F32),
        ),
        in_specs=[ANY, ANY],
        out_specs=(ANY, ANY),
        scratch_shapes=[vmem((heads, HD, HD), F32), vmem((HK, HD, HD), F32), dma((2, OUT_PARTS + 1))],
        compiler_params=pltpu.CompilerParams(vmem_limit_bytes=LIMIT),
        name="store",
    )(gq.reshape(heads, HD, HD), gk.reshape(HK, HD, HD))
    return gq, gk


def solution(mesh):
    placed = (
        P("dp", "seq", None), P("dp", "seq", None), P("dp", "seq", None), P("dp", "seq", None),
        P(), P(), P("dp", None),
    )
    return jax.shard_map(shards, mesh=mesh, in_specs=placed, out_specs=(P(), P()), check_vma=False)
```

```python
import functools
import math

import jax
import jax.numpy as jnp
from jax import lax
from jax.experimental import pallas as pl
from jax.experimental.pallas import tpu as pltpu
from jax.sharding import PartitionSpec as P

MESH = pl.DeviceIdType.MESH
F32 = jnp.float32
BF16 = jnp.bfloat16
SPAN = 128
HD = 128
HK = 4
GROUP = 8
NDOC = 8
NZ = 8
NY = 4
NDP = 8
ZROW = 256
FIRST, LAST = 0, HK - 1


def dot(a, b, ca, cb):
    return lax.dot_general(a, b, (((ca,), (cb,)), ((), ())), preferred_element_type=F32)


def starts_of(spans_ref):
    starts, total = [], jnp.int32(0)
    for n in range(NDOC):
        starts.append(total)
        total = total + spans_ref[0, n]
    return starts


def no_start(starts, *blocks):
    hit = jnp.bool_(False)
    for s in starts:
        for b in blocks:
            hit = jnp.logical_or(hit, s == b)
    return jnp.where(hit, 0.0, 1.0).astype(F32)


def softmax_pair(u):
    e1 = jnp.exp(u - jnp.max(u, -1, keepdims=True))
    e2 = jnp.exp(jnp.min(u, -1, keepdims=True) - u)
    p1 = e1 * (1.0 / jnp.sum(e1, -1, keepdims=True))
    p2 = e2 * (1.0 / jnp.sum(e2, -1, keepdims=True))
    return p1, p2


def map_grad(p1, p2, d1, d2):
    s1 = jnp.sum(p1 * d1, -1, keepdims=True)
    s2 = jnp.sum(p2 * d2, -1, keepdims=True)
    return (p1 * (d1 - s1) - p2 * (d2 - s2)).astype(BF16)


def softmax_pair_t(u):
    e1 = jnp.exp(u - jnp.max(u, 0, keepdims=True))
    e2 = jnp.exp(jnp.min(u, 0, keepdims=True) - u)
    p1 = e1 * (1.0 / jnp.sum(e1, 0, keepdims=True))
    p2 = e2 * (1.0 / jnp.sum(e2, 0, keepdims=True))
    return p1, p2


def remote(src, dst, send, recv, dev):
    return pltpu.make_async_remote_copy(
        src_ref=src, dst_ref=dst, send_sem=send, recv_sem=recv, device_id=dev, device_id_type=MESH
    )


def send_all(items):
    copies = [remote(*item) for item in items]
    for copy in copies:
        copy.start()
    return copies


def rows_of(index, size):
    return pl.ds(pl.multiple_of(index * size, 8), size)


def slice_rows(head, holder):
    return 40 if head == holder else 32


def scan_scratch(holder):
    shapes = []
    for head in range(HK):
        size = slice_rows(head, holder)
        shapes += [
            pltpu.VMEM((NZ * size, 128), F32),
            pltpu.VMEM((NZ * size, 128), F32),
            pltpu.VMEM((NZ, size, 128), F32),
            pltpu.VMEM((size, 128), F32),
            pltpu.VMEM((2, size, 128), F32),
            pltpu.VMEM((NZ, size, 128), F32),
            pltpu.SemaphoreType.DMA((2, NZ)),
            pltpu.SemaphoreType.DMA((2, 2)),
            pltpu.SemaphoreType.DMA((2, NZ)),
        ]
    return shapes


class Scan:
    def __init__(self, at, co, scratch, size, reverse):
        self.co, self.size, self.reverse = co, size, reverse
        self.own, self.out, self.seen, self.total, self.rows_in, self.back = scratch[:6]
        self.s1, self.s2, self.s3 = scratch[6:]
        self.dp, self.seq, self.y, self.z = at
        self.order = list(range(NZ))[::-1] if reverse else list(range(NZ))

    def start(self):
        self.copies = send_all([
            (
                self.own.at[rows_of(lax.rem(self.z + d, NZ), self.size)], self.seen.at[self.z],
                self.s1.at[0, d], self.s1.at[1, d], (self.dp, self.y * NZ + lax.rem(self.z + d, NZ)),
            )
            for d in range(1, NZ)
        ])

    def totals(self):
        self.seen[self.z] = self.own[rows_of(self.z, self.size), :]
        for copy in self.copies:
            copy.wait_recv()
        acc = jnp.zeros((self.size, 128), F32)
        for k in self.order:
            self.back[k] = acc
            acc = self.seen[k] + self.co[k : k + 1, :] * acc
        self.total[...] = acc
        self.row_copies = send_all([
            (
                self.total, self.rows_in.at[d - 1], self.s2.at[0, d - 1], self.s2.at[1, d - 1],
                (self.dp, lax.rem(self.y + (NY - d if self.reverse else d), NY) * NZ + self.z),
            )
            for d in (1, 2)
        ])

    def give_back(self):
        for copy in self.row_copies:
            copy.wait_recv()
        first = 10 if self.reverse else 8
        carry = (
            self.co[first : first + 1, :] * self.rows_in[0]
            + self.co[first + 1 : first + 2, :] * self.rows_in[1]
        )
        keep = jnp.ones((1, 128), F32)
        for k in self.order:
            self.back[k] = self.back[k] + keep * carry
            keep = keep * self.co[k : k + 1, :]
        self.out[rows_of(self.z, self.size), :] = self.back[self.z]
        self.back_copies = send_all([
            (
                self.back.at[lax.rem(self.z + d, NZ)], self.out.at[rows_of(self.z, self.size)],
                self.s3.at[0, d], self.s3.at[1, d], (self.dp, self.y * NZ + lax.rem(self.z + d, NZ)),
            )
            for d in range(1, NZ)
        ])

    def arrived(self):
        for copy in self.back_copies:
            copy.wait_recv()

    def sent(self):
        return self.copies + self.row_copies + self.back_copies


def sum_scratch():
    dma = pltpu.SemaphoreType.DMA
    return [
        pltpu.VMEM((1024, 128), F32), pltpu.VMEM((1024, 128), F32), pltpu.VMEM((16, 64, 128), F32),
        pltpu.VMEM((64, 128), F32), pltpu.VMEM((NZ, 8, 128), F32),
        dma((2,)), dma((2, 16)), dma((2, NZ)), dma((2, NZ)), dma((2, 16)), dma((2,)),
    ]


class Total:
    def __init__(self, at, part, source, out, scratch, mate, planes, zs):
        self.source, self.out = source, out
        self.half_in, self.half, self.xy_in, self.quarter, self.z_in = scratch[:5]
        self.sc, self.sxy, self.sz, self.az, self.axy, self.ac = scratch[5:]
        self.mate, self.planes, self.zs = mate, planes, zs
        self.dp, self.seq, self.y, self.z = at
        self.x, self.core = lax.div(self.dp, 2), lax.rem(self.dp, 2)
        self.low = part * 2048
        self.base = self.low + self.core * 1024 + (self.x * 4 + self.y) * 64

    def core_rows(self, core):
        return pl.ds(pl.multiple_of(self.low + core * 1024, 8), 1024)

    def pair(self):
        self.c1 = send_all([
            (self.source.at[self.core_rows(1 - self.core)], self.half_in, self.sc.at[0], self.sc.at[1], self.mate)
        ])

    def plane(self):
        self.c1[0].wait_recv()
        self.half[...] = self.source[self.core_rows(self.core), :] + self.half_in[...]
        items = []
        for d in range(1, 16):
            spot = lax.rem(self.x + d // 4, 4) * 4 + lax.rem(self.y + d % 4, 4)
            items.append((
                self.half.at[rows_of(spot, 64)], self.xy_in.at[d], self.sxy.at[0, d], self.sxy.at[1, d],
                self.planes[d - 1],
            ))
        self.c2 = send_all(items)

    def along_z(self):
        for copy in self.c2:
            copy.wait_recv()
        acc = self.half[rows_of(self.x * 4 + self.y, 64), :]
        for d in range(1, 16):
            acc = acc + self.xy_in[d]
        self.quarter[...] = acc
        self.c3 = send_all([
            (
                self.quarter.at[rows_of(lax.rem(self.z + d, NZ), 8)], self.z_in.at[d],
                self.sz.at[0, d], self.sz.at[1, d], self.zs[d - 1],
            )
            for d in range(1, NZ)
        ])

    def back_z(self):
        for copy in self.c3:
            copy.wait_recv()
        acc = self.quarter[rows_of(self.z, 8), :]
        for d in range(1, NZ):
            acc = acc + self.z_in[d]
        mine = pl.ds(pl.multiple_of(self.base + self.z * 8, 8), 8)
        self.out[mine, :] = acc
        self.c4 = send_all([
            (self.out.at[mine], self.out.at[mine], self.az.at[0, d], self.az.at[1, d], self.zs[d - 1])
            for d in range(1, NZ)
        ])

    def back_plane(self):
        for copy in self.c4:
            copy.wait_recv()
        block = pl.ds(pl.multiple_of(self.base, 8), 64)
        self.c5 = send_all([
            (self.out.at[block], self.out.at[block], self.axy.at[0, d], self.axy.at[1, d], self.planes[d - 1])
            for d in range(1, 16)
        ])

    def back_pair(self):
        for copy in self.c5:
            copy.wait_recv()
        whole = self.core_rows(self.core)
        self.c6 = send_all([(self.out.at[whole], self.out.at[whole], self.ac.at[0], self.ac.at[1], self.mate)])

    def arrived(self):
        self.c6[0].wait_recv()

    def sent(self):
        return self.c1 + self.c2 + self.c3 + self.c4 + self.c5 + self.c6


N_SCAN = 9 * HK
N_SUM = 11


def whole_kernel(
    coef, spans_ref, q_hbm, k_ref, v_ref, t_hbm, w_hbm, wk_ref, oq_ref, ok_ref,
    q_s, t_s, w_s, fk_s, pk_s, st0_s, st0z_s, co_s, p_s, f_s, x_s, m_s, both_s, d_s, acc_s, gq_s, den_s, num_s,
    gk, kd_in, ky, kz_in, load, skd, skz, akd, *scratch,
):
    dp, seq = lax.axis_index("dp"), lax.axis_index("seq")
    y, z = lax.div(seq, NZ), lax.rem(seq, NZ)
    at = (dp, seq, y, z)
    x, core = lax.div(dp, 2), lax.rem(dp, 2)
    mate = (x * 2 + (1 - core), seq)
    zs = [(dp, y * NZ + lax.rem(z + d, NZ)) for d in range(1, NZ)]
    planes = [
        (lax.rem(x + d // 4, 4) * 2 + core, lax.rem(y + d % 4, 4) * NZ + z) for d in range(1, 16)
    ]
    layer = [
        (lax.rem(dp + d // NY, NDP), lax.rem(y + d % NY, NY) * NZ + z) for d in range(1, NDP * NY)
    ]
    peers = zs + layer
    barrier = pltpu.get_barrier_semaphore()
    for dev in peers:
        pl.semaphore_signal(barrier, inc=1, device_id=dev, device_id_type=MESH)

    loads = []
    for h in range(HK):
        lanes = pl.ds(h * GROUP * HD, GROUP * HD)
        maps = pl.ds(h * GROUP, GROUP)
        loads.append([
            pltpu.make_async_copy(q_hbm.at[:, lanes], q_s.at[:, lanes], load.at[0, h]),
            pltpu.make_async_copy(w_hbm.at[maps], w_s.at[maps], load.at[1, h]),
            pltpu.make_async_copy(t_hbm.at[:, lanes], t_s.at[:, lanes], load.at[2, h]),
        ])
    for kind in range(3):
        for h in range(HK):
            loads[h][kind].start()

    starts = starts_of(spans_ref)
    b0 = 2 * seq
    in0 = no_start(starts, b0)
    same = no_start(starts, b0 + 1)
    in1 = no_start(starts, b0, b0 + 1)
    out0 = no_start(starts, b0 + 1, b0 + 2)
    out1 = no_start(starts, b0 + 2)
    halves = [(0, slice(0, 128)), (1, slice(128, 256))]

    fwd = [
        Scan(at, co_s, scratch[9 * h : 9 * h + 9], slice_rows(h, FIRST), False) for h in range(HK)
    ]
    rest = scratch[N_SCAN:]
    rev = [Scan(at, co_s, rest[9 * h : 9 * h + 9], slice_rows(h, LAST), True) for h in range(HK)]
    rest = rest[N_SCAN:]
    sums = [
        Total(at, p, gq_s, oq_ref, rest[N_SUM * p : N_SUM * p + N_SUM], mate, planes, zs) for p in (0, 1)
    ]

    fwd[FIRST].own[pl.ds(ZROW, 64), :] = jnp.zeros((64, 128), F32)
    rev[LAST].own[pl.ds(ZROW, 64), :] = jnp.zeros((64, 128), F32)
    for h in range(HK):
        cols = slice(h * HD, (h + 1) * HD)
        p1, p2 = softmax_pair(dot(k_ref[:, cols], wk_ref[h], 1, 0))
        pk_s[0, :, cols] = p1
        pk_s[1, :, cols] = p2
        fk = jnp.concatenate([p1, p2], -1).astype(BF16)
        fk_s[:, h * 256 : (h + 1) * 256] = fk
        v = v_ref[:, cols]
        toks = [slice(c * SPAN, (c + 1) * SPAN) for c in (0, 1)]
        st = [dot(v[r], fk[r], 0, 0) for r in toks]
        zsum = [jnp.sum(fk[r].astype(F32), 0, keepdims=True) for r in toks]
        for half, lanes in halves:
            rows = slice(half * 128, (half + 1) * 128)
            st0_s[h, rows, :] = st[0][:, lanes]
            fwd[h].own[rows, :] = same * st[0][:, lanes] + st[1][:, lanes]
            n = 2 * h + half
            st0z_s[n : n + 1, :] = zsum[0][:, lanes]
            fwd[FIRST].own[ZROW + n : ZROW + n + 1, :] = same * zsum[0][:, lanes] + zsum[1][:, lanes]
    pos = lax.broadcasted_iota(jnp.int32, (NZ, 128), 0) + y * NZ
    hit = jnp.zeros((NZ, 128), F32)
    before, after = jnp.float32(1.0), jnp.float32(1.0)
    for s in starts:
        hit = jnp.where(pos == s // 2, 1.0, hit)
        before = jnp.where(s // 16 == y - 1, 0.0, before)
        after = jnp.where(s // 16 == y + 1, 0.0, after)
    co_s[0:8, :] = 1.0 - hit
    co_s[8:9, :] = jnp.full((1, 128), jnp.where(y >= 1, 1.0, 0.0), F32)
    co_s[9:10, :] = jnp.full((1, 128), jnp.where(y >= 2, before, 0.0), F32)
    co_s[10:11, :] = jnp.full((1, 128), jnp.where(y <= 2, 1.0, 0.0), F32)
    co_s[11:12, :] = jnp.full((1, 128), jnp.where(y <= 1, after, 0.0), F32)

    pl.semaphore_wait(barrier, len(peers))
    for h in range(HK):
        fwd[h].start()

    def features(h):
        loads[h][0].wait()
        loads[h][1].wait()
        for g in range(GROUP):
            cols = slice((h * GROUP + g) * HD, (h * GROUP + g + 1) * HD)
            spot = slice(g * SPAN, (g + 1) * SPAN)
            p1, p2 = softmax_pair_t(dot(w_s[h * GROUP + g], q_s[:, cols], 0, 1))
            for c in (0, 1):
                toks = slice(c * SPAN, (c + 1) * SPAN)
                f_s[2 * h + c, 0:128, spot] = p1[:, toks].astype(BF16)
                f_s[2 * h + c, 128:256, spot] = p2[:, toks].astype(BF16)
                p_s[2 * h + c, 0, :, spot] = p1[:, toks]
                p_s[2 * h + c, 1, :, spot] = p2[:, toks]

    top = lax.broadcasted_iota(jnp.int32, (16, 128), 0)
    down = lax.broadcasted_iota(jnp.int32, (SPAN, SPAN), 0)
    across = lax.broadcasted_iota(jnp.int32, (SPAN, SPAN), 1)
    causal = down <= across
    eye = (down == across).astype(F32).astype(BF16)

    def local(h):
        def one_block(c, carry):
            toks = pl.ds(pl.multiple_of(c * SPAN, SPAN), SPAN)
            ic = 2 * h + c
            both_s[0:128, :] = dot(fk_s[toks, h * 256 : (h + 1) * 256], f_s[ic], 1, 0)
            for g in range(GROUP):
                spot = slice(g * SPAN, (g + 1) * SPAN)
                scores = jnp.where(causal, both_s[0:128, spot], 0.0)
                x_s[ic, 0:128, spot] = scores.astype(BF16)
                den_s[ic, 0:1, spot] = jnp.sum(scores, 0, keepdims=True)
            num_s[ic] = dot(v_ref[toks, h * HD : (h + 1) * HD], x_s[ic, 0:128, :], 0, 0)
            return carry

        lax.fori_loop(0, 2, one_block, 0)

    def front(h):
        loads[h][2].wait()

        def one_block(c, carry):
            w_in = jnp.where(c == 0, in0, in1)
            w_st = jnp.where(c == 0, 0.0, same)
            toks = pl.ds(pl.multiple_of(c * SPAN, SPAN), SPAN)
            ic = 2 * h + c
            m_s[ic, 0:128, :] = fk_s[toks, h * 256 : (h + 1) * 256]
            for half, lanes in halves:
                rows = slice(half * 128, (half + 1) * 128)
                m_s[ic, 128:256, lanes] = (w_in * fwd[h].out[rows, :] + w_st * st0_s[h, rows, :]).astype(BF16)
                n = 2 * h + half
                zb = w_in * fwd[FIRST].out[ZROW + n : ZROW + n + 1, :] + w_st * st0z_s[n : n + 1, :]
                m_s[ic, 256:272, lanes] = jnp.where(top == 0, zb, 0.0).astype(BF16)
            v = v_ref[toks, h * HD : (h + 1) * HD]
            both_s[128:272, :] = dot(m_s[ic, 128:272, :], f_s[ic], 1, 0)
            for g in range(GROUP):
                cols = slice((h * GROUP + g) * HD, (h * GROUP + g + 1) * HD)
                spot = slice(g * SPAN, (g + 1) * SPAN)
                inv = 1.0 / (den_s[ic, 0:1, spot] + both_s[256:257, spot])
                out = (num_s[ic, :, spot] + both_s[128:256, spot]) * inv
                dy = coef * (out - dot(eye, t_s[toks, cols], 1, 1))
                x_s[ic, 128:256, spot] = (dy * inv).astype(BF16)
                dden = -jnp.sum(dy * out, 0, keepdims=True) * inv
                den_s[ic, 1:2, spot] = dden
                hi = dden.astype(BF16).astype(F32)
                mid = (dden - hi).astype(BF16).astype(F32)
                low = dden - hi - mid
                x_s[ic, 256:272, spot] = jnp.where(
                    top == 0, hi, jnp.where(top == 1, mid, jnp.where(top == 2, low, 0.0))
                ).astype(BF16)
            both_s[0:128, :] = dot(v, x_s[ic, 128:256, :], 1, 0)
            for g in range(GROUP):
                spot = slice(g * SPAN, (g + 1) * SPAN)
                x_s[ic, 0:128, spot] = jnp.where(causal, both_s[0:128, spot] + den_s[ic, 1:2, spot], 0.0).astype(BF16)
            acc_s[ic] = dot(x_s[ic], f_s[ic], 1, 1)
            return carry

        lax.fori_loop(0, 2, one_block, 0)
        for half, lanes in halves:
            rows = slice(half * 128, (half + 1) * 128)
            rev[h].own[rows, :] = in0 * acc_s[2 * h, 128:256, lanes] + in1 * acc_s[2 * h + 1, 128:256, lanes]
            gz = [sum_rows(acc_s, 2 * h + c, lanes) for c in (0, 1)]
            n = 2 * h + half
            rev[LAST].own[ZROW + n : ZROW + n + 1, :] = in0 * gz[0] + in1 * gz[1]

    def rear(h):
        def one_block(c, carry):
            ic = 2 * h + c
            zcol = dot(m_s[ic, 256:272, :], jnp.ones((16, 128), BF16), 0, 0)
            both_s[0:256, :] = dot(m_s[ic, 0:256, :], x_s[ic, 0:256, :], 0, 0)
            for g in range(GROUP):
                spot = slice(g * SPAN, (g + 1) * SPAN)
                dden = den_s[ic, 1:2, spot]
                p1, p2 = p_s[ic, 0, :, spot], p_s[ic, 1, :, spot]
                d1 = both_s[0:128, spot] + zcol[0:128] * dden
                d2 = both_s[128:256, spot] + zcol[128:256] * dden
                s1 = jnp.sum(p1 * d1, 0, keepdims=True)
                s2 = jnp.sum(p2 * d2, 0, keepdims=True)
                d_s[c, :, spot] = (p1 * (d1 - s1) - p2 * (d2 - s2)).astype(BF16)
            return carry

        lax.fori_loop(0, 2, one_block, 0)
        for g in range(GROUP):
            n = h * GROUP + g
            cols = slice(n * HD, (n + 1) * HD)
            spot = slice(g * SPAN, (g + 1) * SPAN)
            gq_s[n * HD : (n + 1) * HD, :] = dot(q_s[0:SPAN, cols], d_s[0, :, spot], 0, 1) + dot(
                q_s[SPAN : 2 * SPAN, cols], d_s[1, :, spot], 0, 1
            )

    a, b = sums
    features(0)
    features(1)
    features(2)
    local(0)
    fwd[0].totals()
    features(3)
    fwd[1].totals()
    fwd[0].give_back()
    local(1)
    fwd[2].totals()
    fwd[1].give_back()
    local(2)
    fwd[3].totals()
    fwd[2].give_back()
    local(3)
    fwd[3].give_back()
    fwd[0].arrived()
    front(0)
    rev[0].start()
    rear(0)
    fwd[1].arrived()
    front(1)
    rev[1].start()
    rear(1)
    a.pair()
    fwd[2].arrived()
    front(2)
    rev[2].start()
    a.plane()
    rev[0].totals()
    fwd[3].arrived()
    front(3)
    rev[3].start()
    rear(2)
    rev[1].totals()
    rev[0].give_back()
    rear(3)
    b.pair()
    rev[2].totals()
    rev[1].give_back()
    b.plane()
    a.along_z()
    rev[2].give_back()
    rev[3].totals()
    a.back_z()
    rev[3].give_back()
    b.along_z()
    a.back_plane()
    b.back_z()
    for h in range(HK):
        rev[h].arrived()

    for h in range(HK):
        cols = slice(h * HD, (h + 1) * HD)
        total = jnp.zeros((HD, HD), F32)
        for c in (0, 1):
            toks = slice(c * SPAN, (c + 1) * SPAN)
            grads = []
            for half, lanes in halves:
                rows = slice(half * 128, (half + 1) * 128)
                zr = slice(ZROW + 2 * h + half, ZROW + 2 * h + half + 1)
                r, rz = rev[h].out[rows, :], rev[LAST].out[zr, :]
                if c == 0:
                    r = same * acc_s[2 * h + 1, 128:256, lanes] + out0 * r
                    rz = same * sum_rows(acc_s, 2 * h + 1, lanes) + out0 * rz
                else:
                    r, rz = out1 * r, out1 * rz
                grads.append(
                    acc_s[2 * h + c, 0:128, lanes] + dot(v_ref[toks, cols], r.astype(BF16), 1, 0)
                    + rz.astype(BF16).astype(F32)
                )
            duk = map_grad(pk_s[0, toks, cols], pk_s[1, toks, cols], grads[0], grads[1])
            total = total + dot(k_ref[toks, cols], duk, 0, 0)
        gk[cols, :] = total
    kdsend = send_all([
        (
            gk.at[rows_of(lax.rem(dp + d // NY, NDP) * NY + lax.rem(y + d % NY, NY), 16)], kd_in.at[d],
            skd.at[0, d], skd.at[1, d], layer[d - 1],
        )
        for d in range(1, NDP * NY)
    ])
    a.back_pair()
    for copy in kdsend:
        copy.wait_recv()
    acc = gk[rows_of(dp * NY + y, 16), :]
    for d in range(1, NDP * NY):
        acc = acc + kd_in[d]
    ky[...] = acc
    kz_in[z] = acc
    kzsend = send_all([
        (ky, kz_in.at[z], skz.at[0, d], skz.at[1, d], zs[d - 1]) for d in range(1, NZ)
    ])
    b.back_plane()
    for copy in kzsend:
        copy.wait_recv()
    acc = kz_in[0]
    for n in range(1, NZ):
        acc = acc + kz_in[n]
    kmine = rows_of(dp * NY + y, 16)
    ok_ref[kmine, :] = acc
    kdback = send_all([
        (ok_ref.at[kmine], ok_ref.at[kmine], akd.at[0, d], akd.at[1, d], layer[d - 1])
        for d in range(1, NDP * NY)
    ])
    b.back_pair()
    a.arrived()
    b.arrived()
    for copy in kdback:
        copy.wait_recv()
    for part in fwd + rev + sums:
        for copy in part.sent():
            copy.wait_send()
    for copy in kdsend + kzsend + kdback:
        copy.wait_send()


def sum_rows(acc_s, index, lanes):
    return acc_s[index, 256:257, lanes] + acc_s[index, 257:258, lanes] + acc_s[index, 258:259, lanes]


OUT_PARTS = 8


def store_kernel(a_ref, b_ref, oa_ref, ob_ref, a_s, b_s, sems):
    part = a_s.shape[0] // OUT_PARTS
    pieces = [(a_ref, a_s, oa_ref, pl.ds(n * part, part)) for n in range(OUT_PARTS)]
    pieces.append((b_ref, b_s, ob_ref, pl.ds(0, b_s.shape[0])))
    into = [
        pltpu.make_async_copy(src.at[r], held.at[r], sems.at[0, n])
        for n, (src, held, _, r) in enumerate(pieces)
    ]
    out = [
        pltpu.make_async_copy(held.at[r], dst.at[r], sems.at[1, n])
        for n, (_, held, dst, r) in enumerate(pieces)
    ]
    for copy in into:
        copy.start()
    for n in range(len(pieces)):
        into[n].wait()
        out[n].start()
    for copy in out:
        copy.wait()


VM = pl.BlockSpec(memory_space=pltpu.VMEM)
SM = pl.BlockSpec(memory_space=pltpu.SMEM)
ANY = pl.BlockSpec(memory_space=pl.ANY)
LIMIT = 60 * 1024 * 1024


def shards(queries, keys, values, targets, q_map, k_map, doc_spans):
    toks = queries.shape[1]
    heads = HK * GROUP
    coef = 2.0 / math.sqrt(lax.axis_size("dp") * lax.axis_size("seq") * toks * HD)
    dma = pltpu.SemaphoreType.DMA
    vmem = pltpu.VMEM
    gq, gk = pl.pallas_call(
        functools.partial(whole_kernel, coef),
        out_shape=(
            jax.ShapeDtypeStruct((heads * HD, HD), F32), jax.ShapeDtypeStruct((HK * HD, HD), F32),
        ),
        in_specs=[SM, ANY, VM, VM, ANY, ANY, VM],
        out_specs=(VM, VM),
        scratch_shapes=[
            vmem((toks, heads * HD), BF16),
            vmem((toks, heads * HD), BF16),
            vmem((heads, HD, HD), BF16),
            vmem((toks, HK * 256), BF16),
            vmem((2, toks, HK * HD), F32),
            vmem((HK, 256, 128), F32),
            vmem((8, 128), F32),
            vmem((16, 128), F32),
            vmem((2 * HK, 2, 128, GROUP * SPAN), F32),
            vmem((2 * HK, 256, GROUP * SPAN), BF16),
            vmem((2 * HK, 272, GROUP * SPAN), BF16),
            vmem((2 * HK, 272, 256), BF16),
            vmem((272, GROUP * SPAN), F32),
            vmem((2, HD, GROUP * SPAN), BF16),
            vmem((2 * HK, 272, 256), F32),
            vmem((heads * HD, HD), F32),
            vmem((2 * HK, 8, GROUP * SPAN), F32),
            vmem((2 * HK, HD, GROUP * SPAN), F32),
            vmem((HK * HD, HD), F32),
            vmem((NDP * NY, 16, 128), F32),
            vmem((16, 128), F32),
            vmem((NZ, 16, 128), F32),
            dma((3, HK)),
            dma((2, NDP * NY)), dma((2, NZ)), dma((2, NDP * NY)),
        ] + scan_scratch(FIRST) + scan_scratch(LAST) + sum_scratch() + sum_scratch(),
        compiler_params=pltpu.CompilerParams(
            collective_id=0, has_side_effects=True, vmem_limit_bytes=LIMIT
        ),
        name="whole",
    )(doc_spans, queries[0], keys[0], values[0], targets[0], q_map, k_map)
    gq, gk = pl.pallas_call(
        store_kernel,
        out_shape=(
            jax.ShapeDtypeStruct((heads, HD, HD), F32), jax.ShapeDtypeStruct((HK, HD, HD), F32),
        ),
        in_specs=[ANY, ANY],
        out_specs=(ANY, ANY),
        scratch_shapes=[vmem((heads, HD, HD), F32), vmem((HK, HD, HD), F32), dma((2, OUT_PARTS + 1))],
        compiler_params=pltpu.CompilerParams(vmem_limit_bytes=LIMIT),
        name="store",
    )(gq.reshape(heads, HD, HD), gk.reshape(HK, HD, HD))
    return gq, gk


def solution(mesh):
    placed = (
        P("dp", "seq", None), P("dp", "seq", None), P("dp", "seq", None), P("dp", "seq", None),
        P(), P(), P("dp", None),
    )
    return jax.shard_map(shards, mesh=mesh, in_specs=placed, out_specs=(P(), P()), check_vma=False)
```
